32 devices in a mesh: boot: 4 (over z), tm: 8 (over y, x, core).
Axes of the slice: x: 2, y: 2, z: 4, core: 2. Of those that a mesh axis runs over, the one named last changes fastest.
Arguments:
- recording: bfloat16 [4096, 1024], P('tm'), may hold values from -60 to 60, as said below
- starts: int32 [4, 48], P('boot', 'tm'), may hold values from 0 to 448, as said below
- lengths: int32 [4, 48], P('boot', 'tm'), may hold values from 1 to 64, as said below
- support: int32 [4, 4096], P(None, 'boot'), may hold values 0 or 1
Outputs:
- averaged: float32 [32, 4096], P(None, 'boot')
- residual: float32 [32, 4096], P(None, 'tm')
The draws below stay inside these ranges and needn't reach their ends.
Inputs may be any that keep to these rules, and one draw needn't show every extreme that they name: A shard's values are an autoregressive recording; its values stay within the range. Entry [b, j * 6 + k] starts block k of resample b on time shard j, counted from the shard's first sample; a block ends inside its shard. The 6 lengths of one resample on one time shard sum to at most 384.
All inputs are finite; a program needn't handle non-finite values. No bound on the sum of `support` on one device may be relied on, other than what follows from the above.
Results may differ from the reference program's by a relative error of at most 0.0043.
The reference program's roundings to bfloat16 on the way count: a program that leaves them out, or rounds other values in their place, can miss the bound.
Values may be sent and summed in bfloat16 or wider, within the bound.
No kernel may reach another device: no remote copies, remote signals or barrier semaphores. Data moves between devices by JAX's collectives and lax.ppermute only.
A program may use at most 64 MiB of HBM per device.

```python
import jax
import jax.numpy as jnp
from jax import lax

CHANNEL_COUNT = 1024
LAGS = 4
FEAT = 4096
RESPONSE_COUNT = 32
BOOTS = 4
SEG = 512
NBLK = 6
MOST_LEN = 64
CAP = 384
ITERS = 3
CHEB = 5
SAMPLE_COUNT = 4096
N_TM = 8


def draw_recording(key, part):
    first, second = jax.random.split(jax.random.fold_in(key, 5), 2)
    rate = jnp.exp(jax.random.uniform(first, (CHANNEL_COUNT,), jnp.float32, jnp.log(0.3), jnp.log(0.95)))
    noise = jax.random.normal(second, (SAMPLE_COUNT, CHANNEL_COUNT), jnp.float32)
    keeps = jnp.sqrt(1.0 - rate * rate)

    def advance(before, fresh):
        after = rate * before + keeps * fresh
        return (after, after)
    unused, later = lax.scan(advance, noise[0], noise[1:])
    series = jnp.concatenate([noise[:1], later], axis=0)
    envelope = 1.0 + 2.0 * jnp.arange(SAMPLE_COUNT, dtype=jnp.float32) / max(SAMPLE_COUNT - 1, 1)
    series = series * envelope[:, None]
    return jnp.clip(series, -60.0, 60.0).astype(jnp.bfloat16)


def block_plan(key):
    first, second, third, fourth = jax.random.split(jax.random.fold_in(key, 11), 4)
    ceiling = jax.random.randint(first, (BOOTS, N_TM, 1), MOST_LEN // 4, MOST_LEN + 1)
    raw = jax.random.randint(second, (BOOTS, N_TM, NBLK), 0, 1 << 20)
    sizes = 1 + raw % ceiling
    full_shard = jax.random.randint(third, (BOOTS,), 0, N_TM)
    forced = (jnp.arange(N_TM)[None, :] == full_shard[:, None])[:, :, None]
    sizes = jnp.where(forced, MOST_LEN, sizes)
    begins = jax.random.randint(fourth, (BOOTS, N_TM, NBLK), 0, SEG - MOST_LEN + 1)
    blocks = jnp.arange(NBLK)[None, None, :]
    begins = jnp.where(forced & (blocks == 0), SEG - MOST_LEN, begins)
    begins = jnp.where(forced & (blocks == 1), 0, begins)
    return (begins.reshape(BOOTS, N_TM * NBLK).astype(jnp.int32), sizes.reshape(BOOTS, N_TM * NBLK).astype(jnp.int32))


def draw_starts(key, part):
    return block_plan(key)[0]


def draw_lengths(key, part):
    return block_plan(key)[1]


def place_ends(values, own_key, least, largest):
    longest = values.shape.index(max(values.shape))
    spots = []
    for shift in (0, 1):
        where = [jax.random.randint(jax.random.fold_in(own_key, axis), (), 0, length) for axis, length in enumerate(values.shape)]
        where[longest] = (where[longest] + shift) % values.shape[longest]
        spots.append(tuple(where))
    return values.at[spots[0]].set(least).at[spots[1]].set(largest)


def setup_inputs(seed: int = 0) -> dict:
    arg_keys = jax.random.split(jax.random.key(seed), 5)
    return {
        "recording": draw_recording(jax.random.fold_in(arg_keys[4], 71), 0),
        "starts": draw_starts(jax.random.fold_in(arg_keys[4], 71), 0),
        "lengths": draw_lengths(jax.random.fold_in(arg_keys[4], 71), 0),
        "support": place_ends((jax.random.randint(arg_keys[3], (BOOTS, FEAT), 0, 4) < 1).astype(jnp.int32), jax.random.fold_in(arg_keys[3], 1), 0, 1),
    }


ridge_weight = 4.0
shrink_level = 0.75
epsilon = 1e-05

def bootstrap_rows(window, begins, sizes):
    ends = jnp.cumsum(sizes)
    offsets = ends - sizes
    total = ends[-1]
    rows = jnp.arange(CAP, dtype=jnp.int32)
    member = (rows[:, None] >= offsets[None, :]).astype(jnp.int32)
    which = lax.optimization_barrier(jnp.sum(member, axis=1)) - 1
    picked = (which[:, None] == jnp.arange(NBLK, dtype=jnp.int32)[None, :]).astype(jnp.int32)
    anchor = lax.optimization_barrier(jnp.sum(picked * offsets[None, :], axis=1))
    opening = lax.optimization_barrier(jnp.sum(picked * begins[None, :], axis=1))
    live = rows < total
    times = jnp.where(live, opening + rows - anchor, 0).astype(jnp.int32)
    blocks = [jnp.take(window, times + LAGS - 1 - delay_step, axis=0) for delay_step in range(LAGS)]
    design = jnp.concatenate(blocks, axis=1)
    design = jnp.where(live[:, None], design, jnp.zeros_like(design))
    answer = jnp.take(window[:, :RESPONSE_COUNT], times + LAGS, axis=0)
    answer = jnp.where(live[:, None], answer, jnp.zeros_like(answer))
    return (design, answer.T)

def chebyshev(gram, rhs, bound):
    center = ridge_weight + 0.5 * bound
    radius = 0.5 * bound
    sigma = center / radius
    solution = jnp.zeros_like(rhs)
    remain = rhs
    factor = 1.0 / sigma
    update = rhs / center
    for count in range(CHEB):
        solution = solution + update
        if count + 1 < CHEB:
            applied = ridge_weight * update + jnp.dot(update, gram, precision=lax.Precision.HIGHEST)
            remain = remain - applied
            after = 1.0 / (2.0 * sigma - factor)
            update = after * factor * update + 2.0 * after / radius * remain
            factor = after
    return solution

def prepare(design, answer):
    row_scale = 1.0 / CAP
    cross = jnp.dot(answer, design, preferred_element_type=jnp.float32) * row_scale
    gram = jnp.dot(design, design.T, preferred_element_type=jnp.float32) * row_scale
    bound = jnp.sqrt(jnp.sum(gram * gram))
    return (cross, gram, bound)

def local_solve(design, cross, gram, bound, consensus, dual):
    row_scale = 1.0 / CAP
    target = cross + ridge_weight * (consensus - dual)
    projected = lax.dot_general(target.astype(jnp.bfloat16), design, (((1,), (1,)), ((), ())), preferred_element_type=jnp.float32) * row_scale
    weights = chebyshev(gram, projected, bound)
    back = jnp.dot(weights.astype(jnp.bfloat16), design, preferred_element_type=jnp.float32)
    return (target - back) / ridge_weight

def shrink(mean_value):
    norms = jnp.sqrt(lax.optimization_barrier(jnp.sum(mean_value * mean_value, axis=0)))
    level = shrink_level * jnp.mean(norms)
    return mean_value * (jnp.maximum(norms - level, 0.0) / jnp.maximum(norms, level))[None, :]

def reference(recording, starts, lengths, support):
    values = recording.astype(jnp.float32)
    power = lax.optimization_barrier(jnp.sum(values * values, axis=0))
    scale = 1.0 / jnp.sqrt(power / SAMPLE_COUNT + epsilon)
    scaled_input = (values * scale).astype(jnp.bfloat16)
    extended = jnp.concatenate([jnp.zeros((LAGS, CHANNEL_COUNT), jnp.bfloat16), scaled_input], axis=0)
    shard_ids = jnp.arange(N_TM, dtype=jnp.int32)

    def window_of(shard):
        return lax.dynamic_slice_in_dim(extended, (shard * SEG).astype(jnp.int32), SEG + LAGS, 0)

    def fit_boot(plan):
        begins = plan[0].reshape(N_TM, NBLK)
        sizes = plan[1].reshape(N_TM, NBLK)
        windows = jax.vmap(window_of)(shard_ids)
        design, answer = jax.vmap(bootstrap_rows)(windows, begins, sizes)
        cross, gram, bound = jax.vmap(prepare)(design, answer)
        consensus = jnp.zeros((RESPONSE_COUNT, LAGS * CHANNEL_COUNT), jnp.float32)
        dual = jnp.zeros_like(cross)
        for rounds in range(ITERS):
            local = jax.vmap(local_solve, in_axes=(0, 0, 0, 0, None, 0))(design, cross, gram, bound, consensus, dual)
            mean_value = lax.optimization_barrier(jnp.sum(local + dual, axis=0)) / N_TM
            consensus = shrink(mean_value)
            dual = dual + local - consensus[None]
        return consensus
    estimates = lax.map(fit_boot, (starts, lengths))
    chosen = support.astype(jnp.float32)
    tally = lax.optimization_barrier(jnp.sum(chosen, axis=0))
    averaged = lax.optimization_barrier(jnp.sum(chosen[:, None, :] * estimates, axis=0)) / jnp.maximum(tally, 1.0)[None, :]
    lowered_program = averaged.astype(jnp.bfloat16)
    predicted_output = jnp.zeros((RESPONSE_COUNT, SAMPLE_COUNT), jnp.float32)
    for delay_step in range(LAGS):
        source_program = extended[LAGS - 1 - delay_step:LAGS - 1 - delay_step + SAMPLE_COUNT]
        predicted_output = predicted_output + lax.dot_general(lowered_program[:, delay_step * CHANNEL_COUNT:(delay_step + 1) * CHANNEL_COUNT], source_program, (((1,), (1,)), ((), ())), preferred_element_type=jnp.float32)
    residual = scaled_input[:, :RESPONSE_COUNT].astype(jnp.float32).T - predicted_output
    return (averaged, residual)
```

```python
import functools

import jax
import jax.numpy as jnp
from jax import lax
from jax.experimental import pallas as pl
from jax.experimental.pallas import tpu as pltpu
from jax.sharding import PartitionSpec as P

LAGS = 4
RESPONSE_COUNT = 32
NBLK = 6
CAP = 384
ITERS = 3
CHEB = 5

ridge_weight = 4.0
shrink_level = 0.75
epsilon = 1e-05

MARGIN = 128
HALO = 16


VMEM = pl.BlockSpec(memory_space=pltpu.VMEM)
SMEM = pl.BlockSpec(memory_space=pltpu.SMEM)
f32 = jnp.float32
bf16 = jnp.bfloat16


def swapped(block, axis, distance):
    devices = range(lax.axis_size(axis))
    return lax.ppermute(block, axis, [(i, i ^ distance) for i in devices])


def paired_sum(parts):
    while len(parts) > 1:
        parts = [parts[i] + parts[i + 1] for i in range(0, len(parts), 2)]
    return parts[0]


def chip_parts_sum(block, axis="tm"):
    size = lax.axis_size(axis)
    step = 2
    while step < size:
        reach = min(4, size // step)
        block = paired_sum(
            [block] + [swapped(block, axis, k * step) for k in range(1, reach)]
        )
        step *= reach
    return block


def rotated(values, shift, axis):
    return pltpu.roll(values, shift, axis)


def nt_dot(a, b):
    return lax.dot_general(a, b, (((1,), (1,)), ((), ())), preferred_element_type=f32)


def nn_dot(a, b):
    return jnp.dot(a, b, preferred_element_type=f32)


def split(values):
    high = values.astype(bf16)
    low = (values - high.astype(f32)).astype(bf16)
    return high, low


def gathered_lags(products, samples):
    rows = products.shape[0] // LAGS
    total = None
    for lag in range(LAGS):
        part = rotated(products[lag * rows : (lag + 1) * rows], 1 + lag, 1)
        total = part if total is None else total + part
    return total[:, :samples]


def spread_times_window(values, window):
    width = window.shape[0]
    lagged = jnp.concatenate(
        [rotated(values, width - 1 - lag, 1) for lag in range(LAGS)], axis=0
    )
    high, low = split(lagged)
    both = nn_dot(jnp.concatenate([high, low], axis=0), window)
    return both[: lagged.shape[0]] + both[lagged.shape[0] :]


def padded(values, width):
    rows, samples = values.shape
    return jnp.concatenate([values, jnp.zeros((rows, width - samples), f32)], axis=1)


def chebyshev(high, low, rhs, bound):
    center = ridge_weight + 0.5 * bound
    radius = 0.5 * bound
    sigma = center / radius
    rows = rhs.shape[0]
    answer = jnp.zeros_like(rhs)
    remain = rhs
    factor = 1.0 / sigma
    update = rhs / center
    for count in range(CHEB):
        answer = answer + update
        if count + 1 < CHEB:
            first, second = split(update)
            both = nn_dot(jnp.concatenate([first, second], axis=0), high)
            product = both[:rows] + (both[rows:] + nn_dot(first, low))
            remain = remain - (ridge_weight * update + product)
            after = 1.0 / (2.0 * sigma - factor)
            update = after * factor * update + 2.0 * after / radius * remain
            factor = after
    return answer


def local_step(target, window, high, low, bound, uses):
    samples = high.shape[0]
    width = window.shape[0]
    projected = gathered_lags(nt_dot(target.astype(bf16), window), samples) * (1.0 / CAP)
    weights = chebyshev(high, low, projected, bound)
    kept = padded(weights.astype(bf16).astype(f32), width) * uses
    back = spread_times_window(kept, window)
    return (target - back) / ridge_weight


def store_halves(core, values, state_ref, send_ref, keep_ref):
    state_ref[...] = values
    half = values.shape[0] // 2
    keep_ref[...] = state_ref[pl.ds(pl.multiple_of(core * half, half), half), :]
    send_ref[...] = state_ref[pl.ds(pl.multiple_of((1 - core) * half, half), half), :]


def uses_along(iota, starts_ref, lengths_ref):
    total = jnp.zeros(iota.shape, f32)
    for block in range(NBLK):
        begin = starts_ref[0, block]
        inside = (iota >= begin) & (iota < begin + lengths_ref[0, block])
        total = total + jnp.where(inside, 1.0, 0.0)
    return total


def first_kernel(
    count,
    core_ref,
    starts_ref,
    lengths_ref,
    power_ref,
    recording_ref,
    halo_ref,
    window_ref,
    high_ref,
    low_ref,
    cross_ref,
    bound_ref,
    uses_ref,
    answer_ref,
    state_ref,
    send_ref,
    keep_ref,
):
    samples, channels = recording_ref.shape
    width = window_ref.shape[0]
    scale = 1.0 / jnp.sqrt(power_ref[...] / count + epsilon)
    window_ref[:samples, :] = (recording_ref[...].astype(f32) * scale).astype(bf16)
    window_ref[samples : width - HALO, :] = jnp.zeros((width - HALO - samples, channels), bf16)
    tail = lax.broadcasted_iota(jnp.int32, (HALO, channels), 0) >= HALO - LAGS
    window_ref[width - HALO :, :] = jnp.where(
        tail, halo_ref[...].astype(f32) * scale, 0.0
    ).astype(bf16)
    window = window_ref[...]

    along = uses_along(lax.broadcasted_iota(jnp.int32, (1, width), 1), starts_ref, lengths_ref)
    down = uses_along(
        lax.broadcasted_iota(jnp.int32, (samples, 1), 0), starts_ref, lengths_ref
    )
    uses_ref[...] = along

    pairs = nt_dot(window, window)
    pairs = pairs + rotated(rotated(pairs, 1, 0), 1, 1)
    pairs = pairs + rotated(rotated(pairs, 2, 0), 2, 1)
    gram = rotated(rotated(pairs, 1, 0)[:samples], 1, 1)[:, :samples] * (1.0 / CAP)
    weighted = gram * down
    squares = jnp.sum(weighted * gram, axis=0, keepdims=True) * along[:, :samples]
    bound = jnp.sqrt(jnp.sum(squares, axis=1, keepdims=True))
    bound_ref[...] = jnp.broadcast_to(bound, bound_ref.shape)
    high, low = split(weighted)
    high_ref[...] = high
    low_ref[...] = low

    answer = window_ref[:samples, :128].astype(f32).T[:RESPONSE_COUNT]
    answer_ref[...] = answer
    cross = spread_times_window(padded(answer, width) * along, window) * (1.0 / CAP)
    cross_ref[...] = cross
    local = local_step(cross, window, high, low, bound, along)
    store_halves(core_ref[0], local, state_ref, send_ref, keep_ref)


def column_norms(mean):
    parts = mean.shape[0] // RESPONSE_COUNT
    cube = mean.reshape(parts, RESPONSE_COUNT, mean.shape[1])
    return cube, jnp.sqrt(jnp.sum(cube * cube, axis=1))


def shrunk(cube, norms, level):
    return cube * (jnp.maximum(norms - level, 0.0) / jnp.maximum(norms, level))[:, None, :]


def next_kernel(
    core_ref,
    own_ref,
    other_ref,
    window_ref,
    high_ref,
    low_ref,
    cross_ref,
    bound_ref,
    uses_ref,
    state_ref,
    later_ref,
    send_ref,
    keep_ref,
    mean_ref,
):
    half = own_ref.shape[0]
    core = core_ref[0]
    mean_ref[pl.ds(pl.multiple_of(core * half, half), half), :] = own_ref[...]
    mean_ref[pl.ds(pl.multiple_of((1 - core) * half, half), half), :] = other_ref[...]
    cube, norms = column_norms(mean_ref[...])
    level = shrink_level * (jnp.sum(norms, keepdims=True) / norms.size)
    consensus = shrunk(cube, norms, level).reshape(mean_ref.shape)
    dual = state_ref[...] - consensus
    target = cross_ref[...] + ridge_weight * (consensus - dual)
    local = local_step(
        target,
        window_ref[...],
        high_ref[...],
        low_ref[...],
        bound_ref[:1, :1],
        uses_ref[...],
    )
    store_halves(core, local + dual, later_ref, send_ref, keep_ref)


def last_kernel(
    place_ref, own_ref, other_ref, window_ref, answer_ref, averaged_ref, residual_ref, full_ref
):
    half = own_ref.shape[0]
    core, position = place_ref[0], place_ref[1]
    full_ref[pl.ds(pl.multiple_of(core * half, half), half), :] = own_ref[...]
    full_ref[pl.ds(pl.multiple_of((1 - core) * half, half), half), :] = other_ref[...]
    samples = residual_ref.shape[1]
    forecast = gathered_lags(nt_dot(full_ref[...].astype(bf16), window_ref[...]), samples)
    residual_ref[...] = answer_ref[...] - forecast
    channels = full_ref.shape[1]
    width = averaged_ref.shape[1]
    opening = position * width
    row = pl.multiple_of((opening // channels) * RESPONSE_COUNT, RESPONSE_COUNT)
    if width == channels:
        averaged_ref[...] = full_ref[pl.ds(row, RESPONSE_COUNT), :]
    else:
        column = pl.multiple_of(opening % channels, width)
        averaged_ref[...] = full_ref[pl.ds(row, RESPONSE_COUNT), pl.ds(column, width)]


def shaped(shape, dtype=f32):
    return jax.ShapeDtypeStruct(shape, dtype)


PARAMS = pltpu.CompilerParams(vmem_limit_bytes=32 * 1024 * 1024)


def per_device(recording, starts, lengths, support):
    shards = lax.axis_size("tm")
    boots = lax.axis_size("boot")
    samples, channels = recording.shape
    width = samples + MARGIN
    rows = LAGS * RESPONSE_COUNT
    half = rows // 2
    core = (lax.axis_index("tm") % 2).astype(jnp.int32)
    position = lax.axis_index("boot").astype(jnp.int32)
    place = jnp.stack([core, position])

    values = recording.astype(f32)
    power = jnp.sum(values * values, axis=0, keepdims=True)
    power = power + swapped(power, "tm", 1)
    power = chip_parts_sum(power)
    halo = lax.ppermute(
        recording[samples - HALO :], "tm", [(i, i + 1) for i in range(shards - 1)]
    )

    half_shape = shaped((half, channels))
    full_shape = shaped((rows, channels))
    window, high, low, cross, bound, uses, answer, state, send, keep = pl.pallas_call(
        functools.partial(first_kernel, samples * shards),
        out_shape=(
            shaped((width, channels), bf16),
            shaped((samples, samples), bf16),
            shaped((samples, samples), bf16),
            full_shape,
            shaped((8, 128)),
            shaped((1, width)),
            shaped((RESPONSE_COUNT, samples)),
            full_shape,
            half_shape,
            half_shape,
        ),
        in_specs=[SMEM, SMEM, SMEM, VMEM, VMEM, VMEM],
        out_specs=(VMEM,) * 10,
        compiler_params=PARAMS,
        name="first",
    )(place, starts, lengths, power, recording, halo)

    received = swapped(send, "tm", 1)
    chip = keep + received
    chip, support = lax.optimization_barrier((chip, support.astype(bf16)))
    total = chip_parts_sum(chip)
    parts = [support] + [swapped(support, "boot", d) for d in range(1, boots)]
    mean = total / shards

    stacked = jnp.stack(parts).astype(f32)
    order = jnp.arange(boots, dtype=jnp.int32) ^ position
    blocks = jnp.stack(
        [lax.dynamic_index_in_dim(stacked, order[k], 0, keepdims=False) for k in range(boots)]
    )
    chosen = jnp.transpose(blocks, (1, 0, 2)).reshape(boots, LAGS, channels)
    chosen = lax.dynamic_slice_in_dim(chosen, core * (LAGS // 2), LAGS // 2, 1)
    tally = jnp.sum(chosen, axis=0)
    mine = lax.dynamic_index_in_dim(chosen, position, 0, keepdims=False)

    for _ in range(ITERS - 1):
        other = swapped(mean, "tm", 1)
        state, send, keep = pl.pallas_call(
            next_kernel,
            out_shape=(full_shape, half_shape, half_shape),
            in_specs=[SMEM] + [VMEM] * 9,
            out_specs=(VMEM,) * 3,
            scratch_shapes=[pltpu.VMEM((rows, channels), f32)],
            compiler_params=PARAMS,
            name="next",
        )(place, mean, other, window, high, low, cross, bound, uses, state)
        chip = keep + swapped(send, "tm", 1)
        mean = chip_parts_sum(chip) / shards

    cube, norms = column_norms(mean)
    summed = jnp.sum(norms).reshape(1, 1)
    summed = summed + swapped(summed, "tm", 1)
    level = shrink_level * (summed / (LAGS * channels))
    consensus = shrunk(cube, norms, level)
    weighted = (mine[:, None, :] * consensus).reshape(half, channels).astype(bf16)
    pieces = [weighted] + [swapped(weighted, "boot", d) for d in range(1, boots)]
    added = paired_sum([piece.astype(f32) for piece in pieces])
    averaged = added.reshape(cube.shape) / jnp.maximum(tally, 1.0)[:, None, :]
    averaged = averaged.reshape(half, channels)
    other = swapped(averaged, "tm", 1)
    return pl.pallas_call(
        last_kernel,
        out_shape=(
            shaped((RESPONSE_COUNT, LAGS * channels // boots)),
            shaped((RESPONSE_COUNT, samples)),
        ),
        in_specs=[SMEM] + [VMEM] * 4,
        out_specs=(VMEM,) * 2,
        scratch_shapes=[pltpu.VMEM((rows, channels), f32)],
        compiler_params=PARAMS,
        name="last",
    )(place, averaged, other, window, answer)


def solution(mesh):
    in_specs = (P("tm", None), P("boot", "tm"), P("boot", "tm"), P(None, "boot"))
    out_specs = (P(None, "boot"), P(None, "tm"))
    return jax.shard_map(
        per_device, mesh=mesh, in_specs=in_specs, out_specs=out_specs, check_vma=False
    )
```

```python
import functools

import jax
import jax.numpy as jnp
from jax import lax
from jax.experimental import pallas as pl
from jax.experimental.pallas import tpu as pltpu
from jax.sharding import PartitionSpec as P

LAGS = 4
RESPONSE_COUNT = 32
NBLK = 6
CAP = 384
ITERS = 3
CHEB = 5

ridge_weight = 4.0
shrink_level = 0.75
epsilon = 1e-05

MARGIN = 128
HALO = 16
CHUNKS = 4


VMEM = pl.BlockSpec(memory_space=pltpu.VMEM)
SMEM = pl.BlockSpec(memory_space=pltpu.SMEM)
f32 = jnp.float32
bf16 = jnp.bfloat16


def swapped(block, axis, distance):
    devices = range(lax.axis_size(axis))
    return lax.ppermute(block, axis, [(i, i ^ distance) for i in devices])


def paired_sum(parts):
    while len(parts) > 1:
        parts = [parts[i] + parts[i + 1] for i in range(0, len(parts), 2)]
    return parts[0]


def chip_parts(block, axis="tm", step=2):
    reach = min(4, lax.axis_size(axis) // step)
    return [block] + [swapped(block, axis, k * step) for k in range(1, reach)]


def chip_parts_sum(block, axis="tm"):
    step = 2
    while step < lax.axis_size(axis):
        parts = chip_parts(block, axis, step)
        total = paired_sum([part.astype(f32) for part in parts])
        block = total.astype(block.dtype)
        step *= len(parts)
    return total


def rotated(values, shift, axis):
    return pltpu.roll(values, shift, axis)


def nt_dot(a, b):
    return lax.dot_general(a, b, (((1,), (1,)), ((), ())), preferred_element_type=f32)


def nn_dot(a, b):
    return jnp.dot(a, b, preferred_element_type=f32)


def split(values):
    high = values.astype(bf16)
    low = (values - high.astype(f32)).astype(bf16)
    return high, low


def gathered_lags(products, samples):
    rows = products.shape[0] // LAGS
    total = None
    for lag in range(LAGS):
        part = rotated(products[lag * rows : (lag + 1) * rows], 1 + lag, 1)
        total = part if total is None else total + part
    return total[:, :samples]


def spread_times_window(values, window):
    width = window.shape[0]
    lagged = jnp.concatenate(
        [rotated(values, width - 1 - lag, 1) for lag in range(LAGS)], axis=0
    )
    high, low = split(lagged)
    both = nn_dot(jnp.concatenate([high, low], axis=0), window)
    return both[: lagged.shape[0]] + both[lagged.shape[0] :]


def padded(values, width):
    rows, samples = values.shape
    return jnp.concatenate([values, jnp.zeros((rows, width - samples), f32)], axis=1)


def chebyshev(high, low, rhs, bound):
    center = ridge_weight + 0.5 * bound
    radius = 0.5 * bound
    sigma = center / radius
    rows = rhs.shape[0]
    answer = jnp.zeros_like(rhs)
    remain = rhs
    factor = 1.0 / sigma
    update = rhs / center
    for count in range(CHEB):
        answer = answer + update
        if count + 1 < CHEB:
            first, second = split(update)
            both = nn_dot(jnp.concatenate([first, second], axis=0), high)
            product = both[:rows] + (both[rows:] + nn_dot(first, low))
            remain = remain - (ridge_weight * update + product)
            after = 1.0 / (2.0 * sigma - factor)
            update = after * factor * update + 2.0 * after / radius * remain
            factor = after
    return answer


def local_step(target, window, high, low, bound, uses):
    samples = high.shape[0]
    width = window.shape[0]
    projected = gathered_lags(nt_dot(target.astype(bf16), window), samples) * (1.0 / CAP)
    weights = chebyshev(high, low, projected, bound)
    kept = padded(weights.astype(bf16).astype(f32), width) * uses
    back = spread_times_window(kept, window)
    return (target - back) / ridge_weight


def store_halves(core, values, state_ref, send_ref, keep_ref):
    state_ref[...] = values
    half = values.shape[0] // 2
    keep_ref[...] = state_ref[pl.ds(pl.multiple_of(core * half, half), half), :]
    send_ref[...] = state_ref[pl.ds(pl.multiple_of((1 - core) * half, half), half), :]


def uses_along(iota, starts_ref, lengths_ref):
    total = jnp.zeros(iota.shape, f32)
    for block in range(NBLK):
        begin = starts_ref[0, block]
        inside = (iota >= begin) & (iota < begin + lengths_ref[0, block])
        total = total + jnp.where(inside, 1.0, 0.0)
    return total


def place():
    index = lax.axis_index("tm")
    return lax.rem(index, 2), lax.div(index, 2), lax.axis_index("boot")


def power_kernel(
    starts_ref,
    lengths_ref,
    source_ref,
    recording_ref,
    packet_ref,
    along_ref,
    down_ref,
    sems,
):
    samples, channels = source_ref.shape
    chunk = samples // CHUNKS
    copies = []
    for k in range(CHUNKS):
        piece = pl.ds(k * chunk, chunk)
        copies.append(
            pltpu.make_async_copy(source_ref.at[piece], recording_ref.at[piece], sems.at[k])
        )
        copies[-1].start()
    along_ref[...] = uses_along(
        lax.broadcasted_iota(jnp.int32, along_ref.shape, 1), starts_ref, lengths_ref
    )
    down_ref[...] = uses_along(
        lax.broadcasted_iota(jnp.int32, down_ref.shape, 0), starts_ref, lengths_ref
    )
    total = jnp.zeros((8, channels), f32)
    for k in range(CHUNKS):
        copies[k].wait()
        values = recording_ref[k * chunk : (k + 1) * chunk, :].astype(f32)
        total = total + jnp.sum((values * values).reshape(chunk // 8, 8, channels), axis=0)
    power = jnp.sum(total, axis=0, keepdims=True)
    last = recording_ref[samples - HALO :, :].astype(f32)[HALO - 8 :]
    row = lax.broadcasted_iota(jnp.int32, (8, channels), 0)
    packet_ref[...] = jnp.where(row < 8 - LAGS, power, last)


def merge_kernel(own_ref, other_ref, merged_ref):
    core, _, _ = place()
    own, other = own_ref[...], other_ref[...]
    row = lax.broadcasted_iota(jnp.int32, own.shape, 0)
    merged_ref[...] = jnp.where(row < 8 - LAGS, own + other, jnp.where(core == 1, own, other))


def preceding_rows(refs):
    if len(refs) == 1:
        return refs[0][...]
    core, chip, _ = place()
    other_ref, *chip_refs = refs
    rows = chip_refs[0][...]
    if len(chip_refs) == 3:
        rows = jnp.where(chip == 2, chip_refs[2][...], rows)
    rows = jnp.where(core == 1, other_ref[...], rows)
    return jnp.where(core + chip > 0, rows, 0.0)


def first_kernel(count, parts, halos, *refs):
    part_refs, refs = refs[:parts], refs[parts:]
    halo_refs, refs = refs[:halos], refs[halos:]
    (
        recording_ref,
        along_ref,
        down_ref,
        window_ref,
        high_ref,
        low_ref,
        cross_ref,
        bound_ref,
        answer_ref,
        state_ref,
        send_ref,
        keep_ref,
    ) = refs
    samples, channels = recording_ref.shape
    width = window_ref.shape[0]
    power = paired_sum([ref[:1, :] for ref in part_refs])
    scale = 1.0 / jnp.sqrt(power / count + epsilon)
    window_ref[:samples, :] = (recording_ref[...].astype(f32) * scale).astype(bf16)
    window_ref[samples : width - HALO, :] = jnp.zeros((width - HALO - samples, channels), bf16)
    row = lax.broadcasted_iota(jnp.int32, (8, channels), 0)
    tail = jnp.where(row >= 8 - LAGS, preceding_rows(halo_refs) * scale, 0.0)
    window_ref[width - HALO :, :] = jnp.concatenate(
        [jnp.zeros((HALO - 8, channels), f32), tail], axis=0
    ).astype(bf16)
    window = window_ref[...]

    along = along_ref[...]
    pairs = nt_dot(window, window)
    pairs = pairs + rotated(rotated(pairs, 1, 0), 1, 1)
    pairs = pairs + rotated(rotated(pairs, 2, 0), 2, 1)
    gram = rotated(rotated(pairs, 1, 0)[:samples], 1, 1)[:, :samples] * (1.0 / CAP)
    weighted = gram * down_ref[:, :1]
    squares = jnp.sum(weighted * gram, axis=0, keepdims=True) * along[:, :samples]
    bound = jnp.sqrt(jnp.sum(squares, axis=1, keepdims=True))
    bound_ref[...] = jnp.broadcast_to(bound, bound_ref.shape)
    high, low = split(weighted)
    high_ref[...] = high
    low_ref[...] = low

    answer = window_ref[:samples, :128].astype(f32).T[:RESPONSE_COUNT]
    answer_ref[...] = answer
    cross = spread_times_window(padded(answer, width) * along, window) * (1.0 / CAP)
    cross_ref[...] = cross
    local = local_step(cross, window, high, low, bound, along)
    core, _, _ = place()
    store_halves(core, local, state_ref, send_ref, keep_ref)


def column_norms(mean):
    parts = mean.shape[0] // RESPONSE_COUNT
    cube = mean.reshape(parts, RESPONSE_COUNT, mean.shape[1])
    return cube, jnp.sqrt(jnp.sum(cube * cube, axis=1))


def shrunk(cube, norms, level):
    return cube * (jnp.maximum(norms - level, 0.0) / jnp.maximum(norms, level))[:, None, :]


def join_halves(core, own_ref, other_ref, full_ref):
    half = own_ref.shape[0]
    full_ref[pl.ds(pl.multiple_of(core * half, half), half), :] = own_ref[...]
    full_ref[pl.ds(pl.multiple_of((1 - core) * half, half), half), :] = other_ref[...]


def next_kernel(
    own_ref,
    other_ref,
    window_ref,
    high_ref,
    low_ref,
    cross_ref,
    bound_ref,
    along_ref,
    state_ref,
    later_ref,
    send_ref,
    keep_ref,
    mean_ref,
):
    core, _, _ = place()
    join_halves(core, own_ref, other_ref, mean_ref)
    cube, norms = column_norms(mean_ref[...])
    level = shrink_level * (jnp.sum(norms, keepdims=True) / norms.size)
    consensus = shrunk(cube, norms, level).reshape(mean_ref.shape)
    dual = state_ref[...] - consensus
    target = cross_ref[...] + ridge_weight * (consensus - dual)
    local = local_step(
        target,
        window_ref[...],
        high_ref[...],
        low_ref[...],
        bound_ref[:1, :1],
        along_ref[...],
    )
    store_halves(core, local + dual, later_ref, send_ref, keep_ref)


def norm_kernel(shards, *refs):
    *part_refs, mean_ref, sum_ref = refs
    mean = paired_sum([ref[...].astype(f32) for ref in part_refs]) / shards
    mean_ref[...] = mean
    _, norms = column_norms(mean)
    sum_ref[...] = jnp.broadcast_to(jnp.sum(norms, keepdims=True), sum_ref.shape)


def weigh_kernel(boots, *refs):
    mean_ref, own_ref, other_ref, *refs = refs
    support_refs, (weighted_ref, tally_ref, blocks_ref) = refs[:boots], refs[boots:]
    core, _, position = place()
    cube, norms = column_norms(mean_ref[...])
    lags, _, channels = cube.shape
    level = shrink_level * ((own_ref[:1, :1] + other_ref[:1, :1]) / (LAGS * channels))
    for d in range(boots):
        blocks_ref[lax.bitwise_xor(position, d)] = support_refs[d][...]
    each = channels // blocks_ref.shape[2]
    mine, tally = [], []
    for lag in range(lags):
        blocks = [blocks_ref.at[(core * lags + lag) * each + k] for k in range(each)]
        mine.append(jnp.concatenate([b[pl.ds(position, 1), :] for b in blocks], axis=1))
        tally.append(
            jnp.concatenate([jnp.sum(b[...], axis=0, keepdims=True) for b in blocks], axis=1)
        )
    tally_ref[...] = jnp.concatenate(tally, axis=0)
    chosen = jnp.concatenate(mine, axis=0)[:, None, :]
    weighted_ref[...] = (chosen * shrunk(cube, norms, level)).reshape(mean_ref.shape).astype(bf16)


def average_kernel(*refs):
    *piece_refs, tally_ref, averaged_ref = refs
    added = paired_sum([ref[...].astype(f32) for ref in piece_refs])
    lags = tally_ref.shape[0]
    cube = added.reshape(lags, RESPONSE_COUNT, added.shape[1])
    averaged_ref[...] = (cube / jnp.maximum(tally_ref[...], 1.0)[:, None, :]).reshape(added.shape)


def last_kernel(
    own_ref, other_ref, window_ref, answer_ref, averaged_ref, residual_ref, full_ref
):
    core, _, position = place()
    join_halves(core, own_ref, other_ref, full_ref)
    samples = residual_ref.shape[1]
    forecast = gathered_lags(nt_dot(full_ref[...].astype(bf16), window_ref[...]), samples)
    residual_ref[...] = answer_ref[...] - forecast
    channels = full_ref.shape[1]
    width = averaged_ref.shape[1]
    opening = position * width
    row = pl.multiple_of(lax.div(opening, channels) * RESPONSE_COUNT, RESPONSE_COUNT)
    if width == channels:
        averaged_ref[...] = full_ref[pl.ds(row, RESPONSE_COUNT), :]
    else:
        column = pl.multiple_of(lax.rem(opening, channels), width)
        averaged_ref[...] = full_ref[pl.ds(row, RESPONSE_COUNT), pl.ds(column, width)]


def shaped(shape, dtype=f32):
    return jax.ShapeDtypeStruct(shape, dtype)


def called(kernel, outs, ins, name, scratch=()):
    return pl.pallas_call(
        kernel,
        out_shape=outs,
        in_specs=ins,
        out_specs=jax.tree.map(lambda _: VMEM, outs),
        scratch_shapes=scratch,
        compiler_params=pltpu.CompilerParams(vmem_limit_bytes=32 * 1024 * 1024),
        name=name,
    )


def per_device(recording, starts, lengths, support):
    shards = lax.axis_size("tm")
    boots = lax.axis_size("boot")
    samples, channels = recording.shape
    width = samples + MARGIN
    rows = LAGS * RESPONSE_COUNT
    half = rows // 2
    half_shape = shaped((half, channels))
    full_shape = shaped((rows, channels))

    recording, packet, along, down = called(
        power_kernel,
        (
            shaped((samples, channels), bf16),
            shaped((8, channels)),
            shaped((1, width)),
            shaped((samples, 128)),
        ),
        [SMEM, SMEM, pl.BlockSpec(memory_space=pl.ANY)],
        "power",
        [pltpu.SemaphoreType.DMA((CHUNKS,))],
    )(starts, lengths, recording)
    other = swapped(packet, "tm", 1)
    merged = called(merge_kernel, shaped((8, channels)), [VMEM, VMEM], "merge")(packet, other)
    if shards <= 8:
        powers = chip_parts(merged)
        halos = [other] + powers[1:]
    else:
        powers = [chip_parts_sum(merged)]
        halos = [lax.ppermute(packet, "tm", [(i, i + 1) for i in range(shards - 1)])]

    window, high, low, cross, bound, answer, state, send, keep = called(
        functools.partial(first_kernel, samples * shards, len(powers), len(halos)),
        (
            shaped((width, channels), bf16),
            shaped((samples, samples), bf16),
            shaped((samples, samples), bf16),
            full_shape,
            shaped((8, 128)),
            shaped((RESPONSE_COUNT, samples)),
            full_shape,
            half_shape,
            half_shape,
        ),
        [VMEM] * (len(powers) + len(halos) + 3),
        "first",
    )(*powers, *halos, recording, along, down)

    chip = (keep + swapped(send, "tm", 1)).astype(bf16)
    chip, support = lax.optimization_barrier((chip, support.astype(f32)))
    mean = chip_parts_sum(chip) / shards
    supports = [support] + [swapped(support, "boot", d) for d in range(1, boots)]
    mean, *supports = lax.optimization_barrier((mean, *supports))

    for count in range(1, ITERS):
        other = swapped(mean, "tm", 1)
        state, send, keep = called(
            next_kernel,
            (full_shape, half_shape, half_shape),
            [VMEM] * 9,
            "next",
            [pltpu.VMEM((rows, channels), f32)],
        )(mean, other, window, high, low, cross, bound, along, state)
        chip = (keep + swapped(send, "tm", 1)).astype(bf16)
        if count + 1 < ITERS:
            mean = chip_parts_sum(chip) / shards

    parts = chip_parts(chip) if shards <= 8 else [chip_parts_sum(chip)]
    mean, summed = called(
        functools.partial(norm_kernel, shards),
        (half_shape, shaped((8, 128))),
        [VMEM] * len(parts),
        "norm",
    )(*parts)
    weighted, tally = called(
        functools.partial(weigh_kernel, boots),
        (shaped((half, channels), bf16), shaped((LAGS // 2, channels))),
        [VMEM] * (3 + boots),
        "weigh",
        [pltpu.VMEM((boots,) + support.shape, f32)],
    )(mean, summed, swapped(summed, "tm", 1), *supports)
    pieces = [weighted] + [swapped(weighted, "boot", d) for d in range(1, boots)]
    averaged = called(average_kernel, half_shape, [VMEM] * (boots + 1), "average")(*pieces, tally)
    return called(
        last_kernel,
        (
            shaped((RESPONSE_COUNT, LAGS * channels // boots)),
            shaped((RESPONSE_COUNT, samples)),
        ),
        [VMEM] * 4,
        "last",
        [pltpu.VMEM((rows, channels), f32)],
    )(averaged, swapped(averaged, "tm", 1), window, answer)


def solution(mesh):
    in_specs = (P("tm", None), P("boot", "tm"), P("boot", "tm"), P(None, "boot"))
    out_specs = (P(None, "boot"), P(None, "tm"))
    return jax.shard_map(
        per_device, mesh=mesh, in_specs=in_specs, out_specs=out_specs, check_vma=False
    )
```

```python
import functools

import jax
import jax.numpy as jnp
from jax import lax
from jax.experimental import pallas as pl
from jax.experimental.pallas import tpu as pltpu
from jax.sharding import PartitionSpec as P


LAGS = 4
RESPONSE_COUNT = 32
NBLK = 6
CAP = 384
ITERS = 3
CHEB = 5

ridge_weight = 4.0
shrink_level = 0.75
epsilon = 1e-05

MARGIN = 128
HALO = 16
CHUNKS = 4


VMEM = pl.BlockSpec(memory_space=pltpu.VMEM)
HBM = pl.BlockSpec(memory_space=pltpu.HBM)
f32 = jnp.float32
bf16 = jnp.bfloat16


def swapped(block, axis, distance):
    devices = range(lax.axis_size(axis))
    return lax.ppermute(block, axis, [(i, i ^ distance) for i in devices])


def paired_sum(parts):
    while len(parts) > 1:
        parts = [parts[i] + parts[i + 1] for i in range(0, len(parts), 2)]
    return parts[0]


def chip_parts(block, step=2):
    reach = min(4, lax.axis_size("tm") // step)
    return [block] + [swapped(block, "tm", k * step) for k in range(1, reach)]


def chip_parts_sum(block):
    step = 2
    while step < lax.axis_size("tm"):
        parts = chip_parts(block, step)
        total = paired_sum([part.astype(f32) for part in parts])
        block = total.astype(block.dtype)
        step *= len(parts)
    return total


def rotated(values, shift, axis):
    return pltpu.roll(values, shift, axis)


def nt_dot(a, b):
    return lax.dot_general(a, b, (((1,), (1,)), ((), ())), preferred_element_type=f32)


def nn_dot(a, b):
    return jnp.dot(a, b, preferred_element_type=f32)


def split(values):
    high = values.astype(bf16)
    low = (values - high.astype(f32)).astype(bf16)
    return high, low


def gathered_lags(products, samples):
    rows = products.shape[0] // LAGS
    total = None
    for lag in range(LAGS):
        part = rotated(products[lag * rows : (lag + 1) * rows], 1 + lag, 1)
        total = part if total is None else total + part
    return total[:, :samples]


def spread_times_window(values, window):
    width = window.shape[0]
    lagged = jnp.concatenate(
        [rotated(values, width - 1 - lag, 1) for lag in range(LAGS)], axis=0
    )
    high, low = split(lagged)
    both = nn_dot(jnp.concatenate([high, low], axis=0), window)
    return both[: lagged.shape[0]] + both[lagged.shape[0] :]


def padded(values, width):
    rows, samples = values.shape
    return jnp.concatenate([values, jnp.zeros((rows, width - samples), f32)], axis=1)


def chebyshev(high, low, rhs, bound):
    center = ridge_weight + 0.5 * bound
    radius = 0.5 * bound
    sigma = center / radius
    answer = jnp.zeros_like(rhs)
    remain = rhs
    factor = 1.0 / sigma
    update = rhs / center
    for count in range(CHEB):
        answer = answer + update
        if count + 1 < CHEB:
            product = times_matrix(update, high, low)
            remain = remain - (ridge_weight * update + product)
            after = 1.0 / (2.0 * sigma - factor)
            update = after * factor * update + 2.0 * after / radius * remain
            factor = after
    return answer


def times_matrix(values, high, low):
    rows = values.shape[0]
    first, second = split(values)
    both = nn_dot(jnp.concatenate([first, second], axis=0), high)
    return both[:rows] + (both[rows:] + nn_dot(first, low))


def solving_matrix(weighted, bound):
    center = ridge_weight + 0.5 * bound
    radius = 0.5 * bound
    sigma = center / radius
    factors = [1.0 / sigma]
    for _ in range(CHEB - 1):
        factors.append(1.0 / (2.0 * sigma - factors[-1]))
    ratios = [None] * CHEB + [1.0]
    for k in reversed(range(CHEB)):
        ratios[k] = factors[k] * ratios[k + 1]
    g0, g1, g2, g3, g4, _ = ratios
    b4 = 2.0 * g0 / radius
    b3 = 4.0 * g1 / radius
    b2 = (4.0 * g2 + 2.0 * g0) / radius
    b1 = (4.0 * g3 + 4.0 * g1) / radius
    b0 = (2.0 * g4 + 2.0 * g2 + g0) / radius
    row = lax.broadcasted_iota(jnp.int32, weighted.shape, 0)
    column = lax.broadcasted_iota(jnp.int32, weighted.shape, 1)
    unit = jnp.where(row == column, 1.0, 0.0)
    t1 = unit - weighted * (1.0 / radius)
    high, low = split(t1)
    t2 = 2.0 * (nn_dot(high, high) + (nn_dot(low, high) + nn_dot(high, low))) - unit
    high, low = split(t2)
    first, second = split(b3 * t1 + b4 * t2)
    product = nn_dot(first, high) + (nn_dot(second, high) + nn_dot(first, low))
    return (b0 - b4) * unit + (b1 - b3) * t1 + b2 * t2 + 2.0 * product


def store_halves(core, values, state_ref, send_ref, keep_ref):
    state_ref[...] = values
    half = values.shape[0] // 2
    keep_ref[...] = state_ref[pl.ds(pl.multiple_of(core * half, half), half), :]
    send_ref[...] = state_ref[pl.ds(pl.multiple_of((1 - core) * half, half), half), :]


def uses_along(iota, starts_ref, lengths_ref):
    total = jnp.zeros(iota.shape, f32)
    for block in range(NBLK):
        begin = starts_ref[0, block]
        inside = (iota >= begin) & (iota < begin + lengths_ref[0, block])
        total = total + jnp.where(inside, 1.0, 0.0)
    return total


def place():
    index = lax.axis_index("tm")
    return lax.rem(index, 2), lax.div(index, 2), lax.axis_index("boot")


def power_kernel(
    starts_hbm,
    lengths_hbm,
    source_ref,
    recording_ref,
    packet_ref,
    along_ref,
    down_ref,
    starts_ref,
    lengths_ref,
    sems,
):
    samples, channels = source_ref.shape
    chunk = samples // CHUNKS
    plan = [
        pltpu.make_async_copy(starts_hbm, starts_ref, sems.at[CHUNKS]),
        pltpu.make_async_copy(lengths_hbm, lengths_ref, sems.at[CHUNKS + 1]),
    ]
    for copy in plan:
        copy.start()
    copies = []
    for k in range(CHUNKS):
        piece = pl.ds(k * chunk, chunk)
        copies.append(
            pltpu.make_async_copy(source_ref.at[piece], recording_ref.at[piece], sems.at[k])
        )
        copies[-1].start()
    for copy in plan:
        copy.wait()
    along_ref[...] = uses_along(
        lax.broadcasted_iota(jnp.int32, along_ref.shape, 1), starts_ref, lengths_ref
    )
    down_ref[...] = uses_along(
        lax.broadcasted_iota(jnp.int32, down_ref.shape, 0), starts_ref, lengths_ref
    )
    total = jnp.zeros((8, channels), f32)
    for k in range(CHUNKS):
        copies[k].wait()
        values = recording_ref[k * chunk : (k + 1) * chunk, :].astype(f32)
        total = total + jnp.sum((values * values).reshape(chunk // 8, 8, channels), axis=0)
    power = jnp.sum(total, axis=0, keepdims=True)
    last = recording_ref[samples - HALO :, :].astype(f32)[HALO - 8 :]
    row = lax.broadcasted_iota(jnp.int32, (8, channels), 0)
    packet_ref[...] = jnp.where(row < 8 - LAGS, power, last)


def merge_kernel(own_ref, other_ref, merged_ref):
    core, _, _ = place()
    own, other = own_ref[...], other_ref[...]
    row = lax.broadcasted_iota(jnp.int32, own.shape, 0)
    merged_ref[...] = jnp.where(row < 8 - LAGS, own + other, jnp.where(core == 1, own, other))


def preceding_rows(refs):
    if len(refs) == 1:
        return refs[0][...]
    core, chip, _ = place()
    other_ref, *chip_refs = refs
    rows = chip_refs[0][...]
    if len(chip_refs) == 3:
        rows = jnp.where(chip == 2, chip_refs[2][...], rows)
    rows = jnp.where(core == 1, other_ref[...], rows)
    return jnp.where(core + chip > 0, rows, 0.0)


def first_kernel(count, parts, halos, *refs):
    part_refs, refs = refs[:parts], refs[parts:]
    halo_refs, refs = refs[:halos], refs[halos:]
    (
        recording_ref,
        along_ref,
        down_ref,
        window_ref,
        high_ref,
        low_ref,
        bound_ref,
        answer_ref,
        state_ref,
        send_ref,
        keep_ref,
    ) = refs
    samples, channels = recording_ref.shape
    width = window_ref.shape[0]
    power = paired_sum([ref[:1, :] for ref in part_refs])
    scale = 1.0 / jnp.sqrt(power / count + epsilon)
    window_ref[:samples, :] = (recording_ref[...].astype(f32) * scale).astype(bf16)
    window_ref[samples : width - HALO, :] = jnp.zeros((width - HALO - samples, channels), bf16)
    row = lax.broadcasted_iota(jnp.int32, (8, channels), 0)
    tail = jnp.where(row >= 8 - LAGS, preceding_rows(halo_refs) * scale, 0.0)
    window_ref[width - HALO :, :] = jnp.concatenate(
        [jnp.zeros((HALO - 8, channels), f32), tail], axis=0
    ).astype(bf16)
    window = window_ref[...]

    along = along_ref[...]
    pairs = nt_dot(window, window)
    pairs = pairs + rotated(rotated(pairs, 1, 0), 1, 1)
    pairs = pairs + rotated(rotated(pairs, 2, 0), 2, 1)
    gram = rotated(rotated(pairs, 1, 0)[:samples], 1, 1)[:, :samples] * (1.0 / CAP)
    weighted = gram * down_ref[:, :1]
    squares = jnp.sum(weighted * gram, axis=0, keepdims=True) * along[:, :samples]
    bound = jnp.sqrt(jnp.sum(squares, axis=1, keepdims=True))
    bound_ref[...] = jnp.broadcast_to(bound, bound_ref.shape)
    high, low = split(weighted)
    high_ref[...] = high
    low_ref[...] = low

    answer = window_ref[:samples, :128].astype(f32).T[:RESPONSE_COUNT]
    answer_ref[...] = answer
    short = answer.astype(bf16)
    projected = (nn_dot(short, high) + nn_dot(short, low)) * (1.0 / CAP)
    weights = chebyshev(high, low, projected, bound).astype(bf16).astype(f32)
    kept = padded(answer * (1.0 / CAP) - weights, width) * along
    local = spread_times_window(kept, window) / ridge_weight
    core, _, _ = place()
    store_halves(core, local, state_ref, send_ref, keep_ref)


def side_kernel(
    window_ref, high_ref, low_ref, bound_ref, answer_ref, along_ref, cross_ref, first_ref, second_ref
):
    width = window_ref.shape[0]
    weighted = high_ref[...].astype(f32) + low_ref[...].astype(f32)
    first_ref[...], second_ref[...] = split(solving_matrix(weighted, bound_ref[:1, :1]))
    answer = padded(answer_ref[...], width) * along_ref[...]
    cross_ref[...] = spread_times_window(answer, window_ref[...]) * (1.0 / CAP)


def column_norms(mean):
    parts = mean.shape[0] // RESPONSE_COUNT
    cube = mean.reshape(parts, RESPONSE_COUNT, mean.shape[1])
    return cube, jnp.sqrt(jnp.sum(cube * cube, axis=1))


def shrunk(cube, norms, level):
    return cube * (jnp.maximum(norms - level, 0.0) / jnp.maximum(norms, level))[:, None, :]


def join_halves(core, own_ref, other_ref, full_ref):
    half = own_ref.shape[0]
    full_ref[pl.ds(pl.multiple_of(core * half, half), half), :] = own_ref[...]
    full_ref[pl.ds(pl.multiple_of((1 - core) * half, half), half), :] = other_ref[...]


def next_kernel(
    own_ref,
    other_ref,
    window_ref,
    first_ref,
    second_ref,
    cross_ref,
    along_ref,
    state_ref,
    later_ref,
    send_ref,
    keep_ref,
    mean_ref,
):
    core, _, _ = place()
    join_halves(core, own_ref, other_ref, mean_ref)
    cube, norms = column_norms(mean_ref[...])
    level = shrink_level * (jnp.sum(norms, keepdims=True) / norms.size)
    consensus = shrunk(cube, norms, level).reshape(mean_ref.shape)
    dual = state_ref[...] - consensus
    target = cross_ref[...] + ridge_weight * (consensus - dual)
    window = window_ref[...]
    samples = first_ref.shape[0]
    projected = gathered_lags(nt_dot(target.astype(bf16), window), samples) * (1.0 / CAP)
    weights = times_matrix(projected, first_ref[...], second_ref[...])
    kept = padded(weights.astype(bf16).astype(f32), window.shape[0]) * along_ref[...]
    local = (target - spread_times_window(kept, window)) / ridge_weight
    store_halves(core, local + dual, later_ref, send_ref, keep_ref)


def norm_kernel(shards, *refs):
    total_ref, *part_refs, mean_ref, sum_ref = refs
    change = paired_sum([ref[...].astype(f32) for ref in part_refs])
    mean = (total_ref[...] + change) / shards
    mean_ref[...] = mean
    _, norms = column_norms(mean)
    sum_ref[...] = jnp.broadcast_to(jnp.sum(norms, keepdims=True), sum_ref.shape)


def weigh_kernel(
    boots, mean_ref, own_ref, other_ref, support_ref, weighted_ref, tally_ref, blocks_ref
):
    core, chip, position = place()
    side = lax.rem(chip, 2)
    start = pl.multiple_of(side * RESPONSE_COUNT, RESPONSE_COUNT)
    cube, norms = column_norms(mean_ref[pl.ds(start, RESPONSE_COUNT), :])
    channels = cube.shape[2]
    level = shrink_level * ((own_ref[:1, :1] + other_ref[:1, :1]) / (LAGS * channels))
    for d in range(boots):
        blocks_ref[lax.bitwise_xor(position, d)] = support_ref[d * boots : (d + 1) * boots, :]
    each = channels // blocks_ref.shape[2]
    blocks = [blocks_ref.at[(core * 2 + side) * each + k] for k in range(each)]
    chosen = jnp.concatenate([b[pl.ds(position, 1), :] for b in blocks], axis=1)
    tally_ref[...] = jnp.concatenate(
        [jnp.sum(b[...], axis=0, keepdims=True) for b in blocks], axis=1
    )
    weighted = chosen[:, None, :] * shrunk(cube, norms, level)
    weighted_ref[...] = weighted.reshape(weighted_ref.shape).astype(bf16)


def average_kernel(*refs):
    *piece_refs, tally_ref, averaged_ref = refs
    added = paired_sum([ref[...].astype(f32) for ref in piece_refs])
    averaged_ref[...] = (added / jnp.maximum(tally_ref[...], 1.0)).astype(bf16)


def last_kernel(*refs):
    *lag_refs, window_ref, answer_ref, averaged_ref, residual_ref, full_ref = refs
    core, chip, position = place()
    mine = core * 2 + lax.rem(chip, 2)
    for step, ref in enumerate(lag_refs):
        lag = lax.bitwise_xor(mine, (step % 2) * 2 + step // 2)
        full_ref[pl.ds(pl.multiple_of(lag * RESPONSE_COUNT, RESPONSE_COUNT), RESPONSE_COUNT), :] = (
            ref[...]
        )
    samples = residual_ref.shape[1]
    forecast = gathered_lags(nt_dot(full_ref[...], window_ref[...]), samples)
    residual_ref[...] = answer_ref[...] - forecast
    channels = full_ref.shape[1]
    width = averaged_ref.shape[1]
    opening = position * width
    row = pl.multiple_of(lax.div(opening, channels) * RESPONSE_COUNT, RESPONSE_COUNT)
    if width == channels:
        block = full_ref[pl.ds(row, RESPONSE_COUNT), :]
    else:
        column = pl.multiple_of(lax.rem(opening, channels), width)
        block = full_ref[pl.ds(row, RESPONSE_COUNT), pl.ds(column, width)]
    averaged_ref[...] = block.astype(f32)


def shaped(shape, dtype=f32):
    return jax.ShapeDtypeStruct(shape, dtype)


def called(kernel, outs, ins, scratch=(), cost=None, room=32):
    return pl.pallas_call(
        kernel,
        cost_estimate=cost,
        out_shape=outs,
        in_specs=ins,
        out_specs=jax.tree.map(lambda _: VMEM, outs),
        scratch_shapes=scratch,
        compiler_params=pltpu.CompilerParams(vmem_limit_bytes=room * 1024 * 1024),
    )


def per_device(recording, starts, lengths, support):
    shards = lax.axis_size("tm")
    boots = lax.axis_size("boot")
    samples, channels = recording.shape
    width = samples + MARGIN
    rows = LAGS * RESPONSE_COUNT
    half = rows // 2
    half_shape = shaped((half, channels))
    full_shape = shaped((rows, channels))

    recording, packet, along, down = called(
        power_kernel,
        (
            shaped((samples, channels), bf16),
            shaped((8, channels)),
            shaped((1, width)),
            shaped((samples, 128)),
        ),
        [HBM] * 3,
        [
            pltpu.SMEM(starts.shape, jnp.int32),
            pltpu.SMEM(lengths.shape, jnp.int32),
            pltpu.SemaphoreType.DMA((CHUNKS + 2,)),
        ],
        room=32,
    )(*[pltpu.with_memory_space_constraint(a, pltpu.HBM) for a in (starts, lengths, recording)])
    other = swapped(packet, "tm", 1)
    merged = called(merge_kernel, shaped((8, channels)), [VMEM, VMEM])(packet, other)
    if shards <= 8:
        powers = chip_parts(merged)
        halos = [other] + powers[1:]
    else:
        powers = [chip_parts_sum(merged)]
        halos = [lax.ppermute(packet, "tm", [(i, i + 1) for i in range(shards - 1)])]

    square = shaped((samples, samples), bf16)
    window, high, low, bound, answer, state, send, keep = called(
        functools.partial(first_kernel, samples * shards, len(powers), len(halos)),
        (
            shaped((width, channels), bf16),
            square,
            square,
            shaped((8, 128)),
            shaped((RESPONSE_COUNT, samples)),
            full_shape,
            half_shape,
            half_shape,
        ),
        [VMEM] * (len(powers) + len(halos) + 3),
    )(*powers, *halos, recording, along, down)

    total = jnp.zeros((half, channels), f32)
    held = total
    support = support.astype(f32)
    reach = 1
    for count in range(1, ITERS):
        change = (keep + swapped(send, "tm", 1) - held).astype(bf16)
        change, support, window, high = lax.optimization_barrier((change, support, window, high))
        total = total + chip_parts_sum(change)
        held = held + change.astype(f32)
        mean = total / shards
        while reach < boots:
            support = jnp.concatenate([support, swapped(support, "boot", reach)], axis=0)
            reach *= 2
            if count + 1 < ITERS:
                break
        if count == 1:
            cross, first, second = called(
                side_kernel,
                (full_shape, square, square),
                [VMEM] * 6,
                cost=pl.CostEstimate(
                    flops=14 * samples**3, bytes_accessed=1 << 20, transcendentals=0
                ),
            )(window, high, low, bound, answer, along)
        mean, support = lax.optimization_barrier((mean, support))
        state, send, keep = called(
            next_kernel,
            (full_shape, half_shape, half_shape),
            [VMEM] * 8,
            [pltpu.VMEM((rows, channels), f32)],
        )(mean, swapped(mean, "tm", 1), window, first, second, cross, along, state)

    change = (keep + swapped(send, "tm", 1) - held).astype(bf16)
    parts = chip_parts(change) if shards <= 8 else [chip_parts_sum(change)]
    mean, summed = called(
        functools.partial(norm_kernel, shards),
        (half_shape, shaped((8, 128))),
        [VMEM] * (1 + len(parts)),
    )(total, *parts)
    lag_shape = shaped((RESPONSE_COUNT, channels), bf16)
    weighted, tally = called(
        functools.partial(weigh_kernel, boots),
        (lag_shape, shaped((1, channels))),
        [VMEM] * 4,
        [pltpu.VMEM((boots, boots, support.shape[1]), f32)],
    )(mean, summed, swapped(summed, "tm", 1), support)
    pieces = [weighted] + [swapped(weighted, "boot", d) for d in range(1, boots)]
    averaged = called(average_kernel, lag_shape, [VMEM] * (boots + 1))(*pieces, tally)
    return called(
        last_kernel,
        (
            shaped((RESPONSE_COUNT, LAGS * channels // boots)),
            shaped((RESPONSE_COUNT, samples)),
        ),
        [VMEM] * 6,
        [pltpu.VMEM((rows, channels), bf16)],
    )(averaged, *[swapped(averaged, "tm", d) for d in range(1, 4)], window, answer)


def solution(mesh):
    in_specs = (P("tm", None), P("boot", "tm"), P("boot", "tm"), P(None, "boot"))
    out_specs = (P(None, "boot"), P(None, "tm"))
    return jax.shard_map(
        per_device,
        mesh=mesh,
        in_specs=in_specs,
        out_specs=out_specs,
        check_vma=False,
    )
```

```python
import functools

import jax
import jax.numpy as jnp
from jax import lax
from jax.experimental import pallas as pl
from jax.experimental.pallas import tpu as pltpu
from jax.sharding import PartitionSpec as P


LAGS = 4
RESPONSE_COUNT = 32
NBLK = 6
CAP = 384
ITERS = 3
CHEB = 5

ridge_weight = 4.0
shrink_level = 0.75
epsilon = 1e-05

MARGIN = 128
HALO = 16
CHUNKS = 4


VMEM = pl.BlockSpec(memory_space=pltpu.VMEM)
HBM = pl.BlockSpec(memory_space=pltpu.HBM)
f32 = jnp.float32
bf16 = jnp.bfloat16


def swapped(block, axis, distance):
    devices = range(lax.axis_size(axis))
    return lax.ppermute(block, axis, [(i, i ^ distance) for i in devices])


def paired_sum(parts):
    while len(parts) > 1:
        parts = [parts[i] + parts[i + 1] for i in range(0, len(parts), 2)]
    return parts[0]


def chip_parts(block, step=2):
    reach = min(4, lax.axis_size("tm") // step)
    return [block] + [swapped(block, "tm", k * step) for k in range(1, reach)]


def chip_parts_sum(block):
    step = 2
    while step < lax.axis_size("tm"):
        parts = chip_parts(block, step)
        total = paired_sum([part.astype(f32) for part in parts])
        block = total.astype(block.dtype)
        step *= len(parts)
    return total


def rotated(values, shift, axis):
    return pltpu.roll(values, shift, axis)


def nt_dot(a, b):
    return lax.dot_general(a, b, (((1,), (1,)), ((), ())), preferred_element_type=f32)


def nn_dot(a, b):
    return jnp.dot(a, b, preferred_element_type=f32)


def split(values):
    high = values.astype(bf16)
    low = (values - high.astype(f32)).astype(bf16)
    return high, low


def gathered_lags(products, samples):
    rows = products.shape[0] // LAGS
    total = None
    for lag in range(LAGS):
        part = rotated(products[lag * rows : (lag + 1) * rows], 1 + lag, 1)
        total = part if total is None else total + part
    return total[:, :samples]


def spread_times_window(values, window):
    width = window.shape[0]
    lagged = jnp.concatenate(
        [rotated(values, width - 1 - lag, 1) for lag in range(LAGS)], axis=0
    )
    high, low = split(lagged)
    both = nn_dot(jnp.concatenate([high, low], axis=0), window)
    return both[: lagged.shape[0]] + both[lagged.shape[0] :]


def padded(values, width):
    rows, samples = values.shape
    return jnp.concatenate([values, jnp.zeros((rows, width - samples), f32)], axis=1)


def chebyshev(high, low, rhs, bound):
    center = ridge_weight + 0.5 * bound
    radius = 0.5 * bound
    sigma = center / radius
    answer = jnp.zeros_like(rhs)
    remain = rhs
    factor = 1.0 / sigma
    update = rhs / center
    for count in range(CHEB):
        answer = answer + update
        if count + 1 < CHEB:
            product = times_matrix(update, high, low)
            remain = remain - (ridge_weight * update + product)
            after = 1.0 / (2.0 * sigma - factor)
            update = after * factor * update + 2.0 * after / radius * remain
            factor = after
    return answer


def times_matrix(values, high, low):
    rows = values.shape[0]
    first, second = split(values)
    both = nn_dot(jnp.concatenate([first, second], axis=0), high)
    return both[:rows] + (both[rows:] + nn_dot(first, low))


def solving_matrix(weighted, bound):
    center = ridge_weight + 0.5 * bound
    radius = 0.5 * bound
    sigma = center / radius
    factors = [1.0 / sigma]
    for _ in range(CHEB - 1):
        factors.append(1.0 / (2.0 * sigma - factors[-1]))
    ratios = [None] * CHEB + [1.0]
    for k in reversed(range(CHEB)):
        ratios[k] = factors[k] * ratios[k + 1]
    g0, g1, g2, g3, g4, _ = ratios
    b4 = 2.0 * g0 / radius
    b3 = 4.0 * g1 / radius
    b2 = (4.0 * g2 + 2.0 * g0) / radius
    b1 = (4.0 * g3 + 4.0 * g1) / radius
    b0 = (2.0 * g4 + 2.0 * g2 + g0) / radius
    row = lax.broadcasted_iota(jnp.int32, weighted.shape, 0)
    column = lax.broadcasted_iota(jnp.int32, weighted.shape, 1)
    unit = jnp.where(row == column, 1.0, 0.0)
    t1 = unit - weighted * (1.0 / radius)
    high, low = split(t1)
    t2 = 2.0 * (nn_dot(high, high) + (nn_dot(low, high) + nn_dot(high, low))) - unit
    high, low = split(t2)
    first, second = split(b3 * t1 + b4 * t2)
    product = nn_dot(first, high) + (nn_dot(second, high) + nn_dot(first, low))
    return (b0 - b4) * unit + (b1 - b3) * t1 + b2 * t2 + 2.0 * product


def store_halves(core, values, state_ref, send_ref, keep_ref):
    state_ref[...] = values
    half = values.shape[0] // 2
    keep_ref[...] = state_ref[pl.ds(pl.multiple_of(core * half, half), half), :]
    send_ref[...] = state_ref[pl.ds(pl.multiple_of((1 - core) * half, half), half), :]


def uses_along(iota, starts_ref, lengths_ref):
    total = jnp.zeros(iota.shape, f32)
    for block in range(NBLK):
        begin = starts_ref[0, block]
        inside = (iota >= begin) & (iota < begin + lengths_ref[0, block])
        total = total + jnp.where(inside, 1.0, 0.0)
    return total


def place():
    index = lax.axis_index("tm")
    return lax.rem(index, 2), lax.div(index, 2), lax.axis_index("boot")


def power_kernel(
    starts_hbm,
    lengths_hbm,
    source_ref,
    recording_ref,
    packet_ref,
    along_ref,
    down_ref,
    starts_ref,
    lengths_ref,
    sems,
):
    samples, channels = source_ref.shape
    chunk = samples // CHUNKS
    plan = [
        pltpu.make_async_copy(starts_hbm, starts_ref, sems.at[CHUNKS]),
        pltpu.make_async_copy(lengths_hbm, lengths_ref, sems.at[CHUNKS + 1]),
    ]
    for copy in plan:
        copy.start()
    copies = []
    for k in range(CHUNKS):
        piece = pl.ds(k * chunk, chunk)
        copies.append(
            pltpu.make_async_copy(source_ref.at[piece], recording_ref.at[piece], sems.at[k])
        )
        copies[-1].start()
    for copy in plan:
        copy.wait()
    along_ref[...] = uses_along(
        lax.broadcasted_iota(jnp.int32, along_ref.shape, 1), starts_ref, lengths_ref
    )
    down_ref[...] = uses_along(
        lax.broadcasted_iota(jnp.int32, down_ref.shape, 0), starts_ref, lengths_ref
    )
    total = jnp.zeros((8, channels), f32)
    for k in range(CHUNKS):
        copies[k].wait()
        values = recording_ref[k * chunk : (k + 1) * chunk, :].astype(f32)
        total = total + jnp.sum((values * values).reshape(chunk // 8, 8, channels), axis=0)
    power = jnp.sum(total, axis=0, keepdims=True)
    last = recording_ref[samples - HALO :, :].astype(f32)[HALO - 8 :]
    row = lax.broadcasted_iota(jnp.int32, (8, channels), 0)
    packet_ref[...] = jnp.where(row < 8 - LAGS, power, last)


def merge_kernel(own_ref, other_ref, merged_ref):
    core, _, _ = place()
    own, other = own_ref[...], other_ref[...]
    row = lax.broadcasted_iota(jnp.int32, own.shape, 0)
    merged_ref[...] = jnp.where(row < 8 - LAGS, own + other, jnp.where(core == 1, own, other))


def preceding_rows(refs):
    if len(refs) == 1:
        return refs[0][...]
    core, chip, _ = place()
    other_ref, *chip_refs = refs
    rows = chip_refs[0][...]
    if len(chip_refs) == 3:
        rows = jnp.where(chip == 2, chip_refs[2][...], rows)
    rows = jnp.where(core == 1, other_ref[...], rows)
    return jnp.where(core + chip > 0, rows, 0.0)


def moved_lanes(blocks, shift):
    turned = [rotated(block, shift, 1) for block in blocks]
    lane = lax.broadcasted_iota(jnp.int32, turned[0].shape, 1)
    return [jnp.where(lane < shift, turned[k - 1], turned[k]) for k in range(len(turned))]


def lagged_gram(window_ref, pairs_ref, sums_ref):
    width = window_ref.shape[0]
    count, rows, lanes = pairs_ref.shape
    samples = rows - HALO
    left = jnp.concatenate([window_ref[width - HALO :, :], window_ref[:samples, :]], axis=0)
    pairs = nt_dot(left, window_ref[...])
    for k in range(count):
        pairs_ref[k] = pairs[:, k * lanes : (k + 1) * lanes]
    body = rows - 8
    earlier = moved_lanes([pairs_ref[k, 7 : 7 + body, :] for k in range(count)], 1)
    for k in range(count):
        sums_ref[k, 8:, :] = pairs_ref[k, 8:, :] + earlier[k]
    first = moved_lanes([sums_ref[k, HALO - 1 : rows - 1, :] for k in range(count)], 1)
    later = moved_lanes([sums_ref[k, HALO - 3 : rows - 3, :] for k in range(count)], 3)
    return jnp.concatenate(
        [first[k] + later[k] for k in range(samples // lanes)], axis=1
    )


def first_kernel(count, parts, halos, *refs):
    part_refs, refs = refs[:parts], refs[parts:]
    halo_refs, refs = refs[:halos], refs[halos:]
    (
        recording_ref,
        along_ref,
        down_ref,
        window_ref,
        high_ref,
        low_ref,
        bound_ref,
        answer_ref,
        state_ref,
        send_ref,
        keep_ref,
        pairs_ref,
        sums_ref,
    ) = refs
    samples, channels = recording_ref.shape
    width = window_ref.shape[0]
    power = paired_sum([ref[:1, :] for ref in part_refs])
    scale = 1.0 / jnp.sqrt(power / count + epsilon)
    window_ref[:samples, :] = (recording_ref[...].astype(f32) * scale).astype(bf16)
    window_ref[samples : width - HALO, :] = jnp.zeros((width - HALO - samples, channels), bf16)
    row = lax.broadcasted_iota(jnp.int32, (8, channels), 0)
    tail = jnp.where(row >= 8 - LAGS, preceding_rows(halo_refs) * scale, 0.0)
    window_ref[width - HALO :, :] = jnp.concatenate(
        [jnp.zeros((HALO - 8, channels), f32), tail], axis=0
    ).astype(bf16)
    window = window_ref[...]

    along = along_ref[...]
    gram = lagged_gram(window_ref, pairs_ref, sums_ref) * (1.0 / CAP)
    weighted = gram * down_ref[:, :1]
    squares = jnp.sum(weighted * gram, axis=0, keepdims=True) * along[:, :samples]
    bound = jnp.sqrt(jnp.sum(squares, axis=1, keepdims=True))
    bound_ref[...] = jnp.broadcast_to(bound, bound_ref.shape)
    high, low = split(weighted)
    high_ref[...] = high
    low_ref[...] = low

    answer = window_ref[:samples, :128].astype(f32).T[:RESPONSE_COUNT]
    answer_ref[...] = answer
    short = answer.astype(bf16)
    projected = (nn_dot(short, high) + nn_dot(short, low)) * (1.0 / CAP)
    weights = chebyshev(high, low, projected, bound).astype(bf16).astype(f32)
    kept = padded(answer * (1.0 / CAP) - weights, width) * along
    local = spread_times_window(kept, window) / ridge_weight
    core, _, _ = place()
    store_halves(core, local, state_ref, send_ref, keep_ref)


def side_kernel(
    window_ref, high_ref, low_ref, bound_ref, answer_ref, along_ref, cross_ref, first_ref, second_ref
):
    width = window_ref.shape[0]
    weighted = high_ref[...].astype(f32) + low_ref[...].astype(f32)
    first_ref[...], second_ref[...] = split(solving_matrix(weighted, bound_ref[:1, :1]))
    answer = padded(answer_ref[...], width) * along_ref[...]
    cross_ref[...] = spread_times_window(answer, window_ref[...]) * (1.0 / CAP)


def column_norms(mean):
    parts = mean.shape[0] // RESPONSE_COUNT
    cube = mean.reshape(parts, RESPONSE_COUNT, mean.shape[1])
    return cube, jnp.sqrt(jnp.sum(cube * cube, axis=1))


def shrunk(cube, norms, level):
    return cube * (jnp.maximum(norms - level, 0.0) / jnp.maximum(norms, level))[:, None, :]


def join_halves(core, own_ref, other_ref, full_ref):
    half = own_ref.shape[0]
    full_ref[pl.ds(pl.multiple_of(core * half, half), half), :] = own_ref[...]
    full_ref[pl.ds(pl.multiple_of((1 - core) * half, half), half), :] = other_ref[...]


def next_kernel(
    own_ref,
    other_ref,
    window_ref,
    first_ref,
    second_ref,
    cross_ref,
    along_ref,
    state_ref,
    send_ref,
    keep_ref,
    *state_refs,
):
    later_ref, mean_ref = state_refs if len(state_refs) == 2 else state_refs * 2
    core, _, _ = place()
    join_halves(core, own_ref, other_ref, mean_ref)
    cube, norms = column_norms(mean_ref[...])
    level = shrink_level * (jnp.sum(norms, keepdims=True) / norms.size)
    consensus = shrunk(cube, norms, level).reshape(mean_ref.shape)
    dual = state_ref[...] - consensus
    target = cross_ref[...] + ridge_weight * (consensus - dual)
    window = window_ref[...]
    samples = first_ref.shape[0]
    projected = gathered_lags(nt_dot(target.astype(bf16), window), samples) * (1.0 / CAP)
    weights = times_matrix(projected, first_ref[...], second_ref[...])
    kept = padded(weights.astype(bf16).astype(f32), window.shape[0]) * along_ref[...]
    local = (target - spread_times_window(kept, window)) / ridge_weight
    store_halves(core, local + dual, later_ref, send_ref, keep_ref)


def part_kernel(boots, own_ref, other_ref, window_ref, support_ref, *refs):
    piece_refs, (tally_ref, full_ref, blocks_ref) = refs[:boots], refs[boots:]
    core, _, position = place()
    join_halves(core, own_ref, other_ref, full_ref)
    cube, norms = column_norms(full_ref[...])
    level = shrink_level * (jnp.sum(norms, keepdims=True) / norms.size)
    for d in range(boots):
        blocks_ref[lax.bitwise_xor(position, d)] = support_ref[d * boots : (d + 1) * boots, :]
    channels = full_ref.shape[1]
    width = blocks_ref.shape[2]
    each = channels // width
    chosen, tally = [], []
    for lag in range(LAGS):
        blocks = [blocks_ref.at[lag * each + k] for k in range(each)]
        chosen.append(jnp.concatenate([b[pl.ds(position, 1), :] for b in blocks], axis=1))
        tally.append(
            jnp.concatenate([jnp.sum(b[...], axis=0, keepdims=True) for b in blocks], axis=1)
        )
    chosen = jnp.concatenate(chosen, axis=0)[:, None, :]
    tally = jnp.maximum(jnp.concatenate(tally, axis=0), 1.0)[:, None, :]
    tally_ref[...] = jnp.sum(blocks_ref[position], axis=0, keepdims=True)
    weighted = chosen * shrunk(cube, norms, level)
    full_ref[...] = weighted.reshape(full_ref.shape)
    share = (weighted / tally).reshape(full_ref.shape).astype(bf16)
    half = RESPONSE_COUNT // 2
    samples = (piece_refs[0].shape[1] - width) // 2
    forecast = gathered_lags(nt_dot(share, window_ref[...]), samples).astype(bf16)
    for d in range(boots):
        opening = lax.bitwise_xor(position, d) * width
        row = lax.div(opening, channels) * RESPONSE_COUNT + core * half
        rows = pl.ds(pl.multiple_of(row, half), half)
        if width == channels:
            block = full_ref[rows, :]
        else:
            column = pl.multiple_of(lax.rem(opening, channels), width)
            block = full_ref[rows, pl.ds(column, width)]
        piece_refs[d][:, :width] = block.astype(bf16)
        piece_refs[d][:, width : width + samples] = forecast[:half]
        piece_refs[d][:, width + samples :] = forecast[half:]


def average_kernel(*refs):
    *piece_refs, tally_ref, answer_ref, averaged_ref, residual_ref = refs
    half, width = averaged_ref.shape
    samples = residual_ref.shape[1]
    added = paired_sum([ref[...].astype(f32) for ref in piece_refs])
    averaged_ref[...] = added[:, :width] / jnp.maximum(tally_ref[...], 1.0)
    residual_ref[:half, :] = answer_ref[:half, :] - added[:, width : width + samples]
    residual_ref[half:, :] = answer_ref[half:, :] - added[:, width + samples :]


def last_kernel(own_ref, other_ref, averaged_ref):
    core, _, _ = place()
    join_halves(core, own_ref, other_ref, averaged_ref)


def shaped(shape, dtype=f32):
    return jax.ShapeDtypeStruct(shape, dtype)


def called(kernel, outs, ins, scratch=(), cost=None, room=32):
    return pl.pallas_call(
        kernel,
        cost_estimate=cost,
        out_shape=outs,
        in_specs=ins,
        out_specs=jax.tree.map(lambda _: VMEM, outs),
        scratch_shapes=scratch,
        compiler_params=pltpu.CompilerParams(vmem_limit_bytes=room * 1024 * 1024),
    )


def per_device(recording, starts, lengths, support):
    shards = lax.axis_size("tm")
    boots = lax.axis_size("boot")
    samples, channels = recording.shape
    width = samples + MARGIN
    rows = LAGS * RESPONSE_COUNT
    half = rows // 2
    half_shape = shaped((half, channels))
    full_shape = shaped((rows, channels))

    recording, packet, along, down = called(
        power_kernel,
        (
            shaped((samples, channels), bf16),
            shaped((8, channels)),
            shaped((1, width)),
            shaped((samples, 128)),
        ),
        [HBM] * 3,
        [
            pltpu.SMEM(starts.shape, jnp.int32),
            pltpu.SMEM(lengths.shape, jnp.int32),
            pltpu.SemaphoreType.DMA((CHUNKS + 2,)),
        ],
        room=32,
    )(*[pltpu.with_memory_space_constraint(a, pltpu.HBM) for a in (starts, lengths, recording)])
    other = swapped(packet, "tm", 1)
    merged = called(merge_kernel, shaped((8, channels)), [VMEM, VMEM])(packet, other)
    if shards <= 8:
        powers = chip_parts(merged)
        halos = [other] + powers[1:]
    else:
        powers = [chip_parts_sum(merged)]
        halos = [lax.ppermute(packet, "tm", [(i, i + 1) for i in range(shards - 1)])]

    square = shaped((samples, samples), bf16)
    window, high, low, bound, answer, state, send, keep = called(
        functools.partial(first_kernel, samples * shards, len(powers), len(halos)),
        (
            shaped((width, channels), bf16),
            square,
            square,
            shaped((8, 128)),
            shaped((RESPONSE_COUNT, samples)),
            full_shape,
            half_shape,
            half_shape,
        ),
        [VMEM] * (len(powers) + len(halos) + 3),
        [pltpu.VMEM((width // 128, samples + HALO, 128), f32)] * 2,
    )(*powers, *halos, recording, along, down)

    total = jnp.zeros((half, channels), f32)
    held = total
    support = support.astype(f32)
    reach = 1
    for count in range(1, ITERS + 1):
        change = (keep + swapped(send, "tm", 1) - held).astype(bf16)
        if count < ITERS:
            change, support, window, high = lax.optimization_barrier(
                (change, support, window, high)
            )
        total = total + chip_parts_sum(change)
        held = held + change.astype(f32)
        mean = total / shards
        if count == ITERS:
            break
        while reach < boots:
            support = jnp.concatenate([support, swapped(support, "boot", reach)], axis=0)
            reach *= 2
            if count + 1 < ITERS:
                break
        if count == 1:
            cross, first, second = called(
                side_kernel,
                (full_shape, square, square),
                [VMEM] * 6,
                cost=pl.CostEstimate(
                    flops=14 * samples**3, bytes_accessed=1 << 20, transcendentals=0
                ),
            )(window, high, low, bound, answer, along)
        mean, support = lax.optimization_barrier((mean, support))
        going = count + 1 < ITERS
        send, keep, *states = called(
            next_kernel,
            (half_shape, half_shape) + (full_shape,) * going,
            [VMEM] * 8,
            [pltpu.VMEM((rows, channels), f32)],
        )(mean, swapped(mean, "tm", 1), window, first, second, cross, along, state)
        state = states[0] if going else None

    features = LAGS * channels // boots
    piece = shaped((RESPONSE_COUNT // 2, features + 2 * samples), bf16)
    *pieces, tally = called(
        functools.partial(part_kernel, boots),
        (piece,) * boots + (shaped((1, features)),),
        [VMEM] * 4,
        [pltpu.VMEM((rows, channels), f32), pltpu.VMEM((boots, boots, features), f32)],
    )(mean, swapped(mean, "tm", 1), window, support)
    pieces = pieces[:1] + [swapped(pieces[d], "boot", d) for d in range(1, boots)]
    averaged, residual = called(
        average_kernel,
        (shaped((RESPONSE_COUNT // 2, features)), shaped((RESPONSE_COUNT, samples))),
        [VMEM] * (boots + 2),
    )(*pieces, tally, answer)
    averaged = called(last_kernel, shaped((RESPONSE_COUNT, features)), [VMEM] * 2)(
        averaged, swapped(averaged, "tm", 1)
    )
    return averaged, residual


def solution(mesh):
    in_specs = (P("tm", None), P("boot", "tm"), P("boot", "tm"), P(None, "boot"))
    out_specs = (P(None, "boot"), P(None, "tm"))
    return jax.shard_map(
        per_device,
        mesh=mesh,
        in_specs=in_specs,
        out_specs=out_specs,
        check_vma=False,
    )
```

```python
import functools

import jax
import jax.numpy as jnp
from jax import lax
from jax.experimental import pallas as pl
from jax.experimental.pallas import tpu as pltpu
from jax.sharding import PartitionSpec as P


LAGS = 4
RESPONSE_COUNT = 32
NBLK = 6
CAP = 384
ITERS = 3
CHEB = 5

ridge_weight = 4.0
shrink_level = 0.75
epsilon = 1e-05

MARGIN = 128
HALO = 16
CHUNKS = 8


VMEM = pl.BlockSpec(memory_space=pltpu.VMEM)
HBM = pl.BlockSpec(memory_space=pltpu.HBM)
f32 = jnp.float32
bf16 = jnp.bfloat16


def swapped(block, axis, distance):
    devices = range(lax.axis_size(axis))
    return lax.ppermute(block, axis, [(i, i ^ distance) for i in devices])


def paired_sum(parts):
    while len(parts) > 1:
        parts = [parts[i] + parts[i + 1] for i in range(0, len(parts), 2)]
    return parts[0]


def chip_parts(block, step=2):
    reach = min(4, lax.axis_size("tm") // step)
    return [block] + [swapped(block, "tm", k * step) for k in range(1, reach)]


def chip_parts_sum(block):
    step = 2
    while step < lax.axis_size("tm"):
        parts = chip_parts(block, step)
        total = paired_sum([part.astype(f32) for part in parts])
        block = total.astype(block.dtype)
        step *= len(parts)
    return total


def rotated(values, shift, axis):
    return pltpu.roll(values, shift, axis)


def nt_dot(a, b):
    return lax.dot_general(a, b, (((1,), (1,)), ((), ())), preferred_element_type=f32)


def nn_dot(a, b):
    return jnp.dot(a, b, preferred_element_type=f32)


def split(values):
    high = values.astype(bf16)
    low = (values - high.astype(f32)).astype(bf16)
    return high, low


def gathered_lags(products, samples):
    rows = products.shape[0] // LAGS
    total = None
    for lag in range(LAGS):
        part = rotated(products[lag * rows : (lag + 1) * rows], 1 + lag, 1)
        total = part if total is None else total + part
    return total[:, :samples]


def spread_times_window(values, window):
    width = window.shape[0]
    lagged = jnp.concatenate(
        [rotated(values, width - 1 - lag, 1) for lag in range(LAGS)], axis=0
    )
    high, low = split(lagged)
    both = nn_dot(jnp.concatenate([high, low], axis=0), window)
    return both[: lagged.shape[0]] + both[lagged.shape[0] :]


def padded(values, width):
    rows, samples = values.shape
    return jnp.concatenate([values, jnp.zeros((rows, width - samples), f32)], axis=1)


def chebyshev(high, low, rhs, bound):
    center = ridge_weight + 0.5 * bound
    radius = 0.5 * bound
    sigma = center / radius
    answer = jnp.zeros_like(rhs)
    remain = rhs
    factor = 1.0 / sigma
    update = rhs / center
    for count in range(CHEB):
        answer = answer + update
        if count + 1 < CHEB:
            product = times_matrix(update, high, low)
            remain = remain - (ridge_weight * update + product)
            after = 1.0 / (2.0 * sigma - factor)
            update = after * factor * update + 2.0 * after / radius * remain
            factor = after
    return answer


def times_matrix(values, high, low):
    rows = values.shape[0]
    first, second = split(values)
    both = nn_dot(jnp.concatenate([first, second], axis=0), high)
    return both[:rows] + (both[rows:] + nn_dot(first, low))


def solving_matrix(weighted, bound):
    center = ridge_weight + 0.5 * bound
    radius = 0.5 * bound
    sigma = center / radius
    factors = [1.0 / sigma]
    for _ in range(CHEB - 1):
        factors.append(1.0 / (2.0 * sigma - factors[-1]))
    ratios = [None] * CHEB + [1.0]
    for k in reversed(range(CHEB)):
        ratios[k] = factors[k] * ratios[k + 1]
    g0, g1, g2, g3, g4, _ = ratios
    b4 = 2.0 * g0 / radius
    b3 = 4.0 * g1 / radius
    b2 = (4.0 * g2 + 2.0 * g0) / radius
    b1 = (4.0 * g3 + 4.0 * g1) / radius
    b0 = (2.0 * g4 + 2.0 * g2 + g0) / radius
    row = lax.broadcasted_iota(jnp.int32, weighted.shape, 0)
    column = lax.broadcasted_iota(jnp.int32, weighted.shape, 1)
    unit = jnp.where(row == column, 1.0, 0.0)
    t1 = unit - weighted * (1.0 / radius)
    high, low = split(t1)
    t2 = 2.0 * (nn_dot(high, high) + (nn_dot(low, high) + nn_dot(high, low))) - unit
    high, low = split(t2)
    first, second = split(b3 * t1 + b4 * t2)
    product = nn_dot(first, high) + (nn_dot(second, high) + nn_dot(first, low))
    return (b0 - b4) * unit + (b1 - b3) * t1 + b2 * t2 + 2.0 * product


def store_halves(core, values, state_ref, send_ref, keep_ref):
    state_ref[...] = values
    half = values.shape[0] // 2
    keep_ref[...] = state_ref[pl.ds(pl.multiple_of(core * half, half), half), :]
    send_ref[...] = state_ref[pl.ds(pl.multiple_of((1 - core) * half, half), half), :]


def uses_along(iota, starts_ref, lengths_ref):
    total = jnp.zeros(iota.shape, f32)
    for block in range(NBLK):
        begin = starts_ref[0, block]
        inside = (iota >= begin) & (iota < begin + lengths_ref[0, block])
        total = total + jnp.where(inside, 1.0, 0.0)
    return total


def place():
    index = lax.axis_index("tm")
    return lax.rem(index, 2), lax.div(index, 2), lax.axis_index("boot")


def power_kernel(
    starts_hbm,
    lengths_hbm,
    source_ref,
    recording_ref,
    packet_ref,
    along_ref,
    down_ref,
    starts_ref,
    lengths_ref,
    sems,
):
    samples, channels = source_ref.shape
    chunk = samples // CHUNKS
    plan = [
        pltpu.make_async_copy(starts_hbm, starts_ref, sems.at[CHUNKS]),
        pltpu.make_async_copy(lengths_hbm, lengths_ref, sems.at[CHUNKS + 1]),
    ]
    for copy in plan:
        copy.start()
    copies = []
    for k in range(CHUNKS):
        piece = pl.ds(k * chunk, chunk)
        copies.append(
            pltpu.make_async_copy(source_ref.at[piece], recording_ref.at[piece], sems.at[k])
        )
        copies[-1].start()
    for copy in plan:
        copy.wait()
    along_ref[...] = uses_along(
        lax.broadcasted_iota(jnp.int32, along_ref.shape, 1), starts_ref, lengths_ref
    )
    down_ref[...] = uses_along(
        lax.broadcasted_iota(jnp.int32, down_ref.shape, 0), starts_ref, lengths_ref
    )
    total = jnp.zeros((8, channels), f32)
    for k in range(CHUNKS):
        copies[k].wait()
        values = recording_ref[k * chunk : (k + 1) * chunk, :].astype(f32)
        total = total + jnp.sum((values * values).reshape(chunk // 8, 8, channels), axis=0)
    power = jnp.sum(total, axis=0, keepdims=True)
    last = recording_ref[samples - HALO :, :].astype(f32)[HALO - 8 :]
    row = lax.broadcasted_iota(jnp.int32, (8, channels), 0)
    packet_ref[...] = jnp.where(row < 8 - LAGS, power, last)


def merge_kernel(own_ref, other_ref, merged_ref):
    core, _, _ = place()
    own, other = own_ref[...], other_ref[...]
    row = lax.broadcasted_iota(jnp.int32, own.shape, 0)
    power = own + other
    first = power.astype(merged_ref.dtype).astype(f32)
    second = (power - first).astype(merged_ref.dtype).astype(f32)
    pieces = jnp.where(row == 0, first, jnp.where(row == 1, second, power - first - second))
    last = jnp.where(core == 1, own, other)
    packet = jnp.where(row < 3, pieces, jnp.where(row < 8 - LAGS, 0.0, last))
    merged_ref[...] = packet.astype(merged_ref.dtype)


def preceding_rows(refs):
    if len(refs) == 1:
        return refs[0][...]
    core, chip, _ = place()
    other_ref, *chip_refs = refs
    rows = chip_refs[0][...].astype(f32)
    if len(chip_refs) == 3:
        rows = jnp.where(chip == 2, chip_refs[2][...].astype(f32), rows)
    rows = jnp.where(core == 1, other_ref[...], rows)
    return jnp.where(core + chip > 0, rows, 0.0)


def moved_lanes(blocks, shift):
    turned = [rotated(block, shift, 1) for block in blocks]
    lane = lax.broadcasted_iota(jnp.int32, turned[0].shape, 1)
    return [jnp.where(lane < shift, turned[k - 1], turned[k]) for k in range(len(turned))]


def lagged_gram(window_ref, pairs_ref, sums_ref):
    width = window_ref.shape[0]
    count, rows, lanes = pairs_ref.shape
    samples = rows - HALO
    left = jnp.concatenate([window_ref[width - HALO :, :], window_ref[:samples, :]], axis=0)
    pairs = nt_dot(left, window_ref[...])
    for k in range(count):
        pairs_ref[k] = pairs[:, k * lanes : (k + 1) * lanes]
    body = rows - 8
    earlier = moved_lanes([pairs_ref[k, 7 : 7 + body, :] for k in range(count)], 1)
    for k in range(count):
        sums_ref[k, 8:, :] = pairs_ref[k, 8:, :] + earlier[k]
    first = moved_lanes([sums_ref[k, HALO - 1 : rows - 1, :] for k in range(count)], 1)
    later = moved_lanes([sums_ref[k, HALO - 3 : rows - 3, :] for k in range(count)], 3)
    return jnp.concatenate(
        [first[k] + later[k] for k in range(samples // lanes)], axis=1
    )


def first_kernel(count, parts, halos, *refs):
    part_refs, refs = refs[:parts], refs[parts:]
    halo_refs, refs = refs[:halos], refs[halos:]
    (
        recording_ref,
        along_ref,
        down_ref,
        window_ref,
        high_ref,
        low_ref,
        bound_ref,
        answer_ref,
        state_ref,
        send_ref,
        keep_ref,
        pairs_ref,
        sums_ref,
    ) = refs
    samples, channels = recording_ref.shape
    width = window_ref.shape[0]
    packets = [ref[...].astype(f32) for ref in part_refs]
    power = paired_sum([packet[:1] + packet[1:2] + packet[2:3] for packet in packets])
    scale = 1.0 / jnp.sqrt(power / count + epsilon)
    window_ref[:samples, :] = (recording_ref[...].astype(f32) * scale).astype(bf16)
    window_ref[samples : width - HALO, :] = jnp.zeros((width - HALO - samples, channels), bf16)
    row = lax.broadcasted_iota(jnp.int32, (8, channels), 0)
    tail = jnp.where(row >= 8 - LAGS, preceding_rows(halo_refs) * scale, 0.0)
    window_ref[width - HALO :, :] = jnp.concatenate(
        [jnp.zeros((HALO - 8, channels), f32), tail], axis=0
    ).astype(bf16)
    window = window_ref[...]

    along = along_ref[...]
    gram = lagged_gram(window_ref, pairs_ref, sums_ref) * (1.0 / CAP)
    weighted = gram * down_ref[:, :1]
    squares = jnp.sum(weighted * gram, axis=0, keepdims=True) * along[:, :samples]
    bound = jnp.sqrt(jnp.sum(squares, axis=1, keepdims=True))
    bound_ref[...] = jnp.broadcast_to(bound, bound_ref.shape)
    high, low = split(weighted)
    high_ref[...] = high
    low_ref[...] = low

    answer = window_ref[:samples, :128].astype(f32).T[:RESPONSE_COUNT]
    answer_ref[...] = answer
    short = answer.astype(bf16)
    projected = (nn_dot(short, high) + nn_dot(short, low)) * (1.0 / CAP)
    weights = chebyshev(high, low, projected, bound).astype(bf16).astype(f32)
    kept = padded(answer * (1.0 / CAP) - weights, width) * along
    local = spread_times_window(kept, window) / ridge_weight
    core, _, _ = place()
    store_halves(core, local, state_ref, send_ref, keep_ref)


def side_kernel(
    window_ref, high_ref, low_ref, bound_ref, answer_ref, along_ref, cross_ref, first_ref, second_ref
):
    width = window_ref.shape[0]
    weighted = high_ref[...].astype(f32) + low_ref[...].astype(f32)
    first_ref[...], second_ref[...] = split(solving_matrix(weighted, bound_ref[:1, :1]))
    answer = padded(answer_ref[...], width) * along_ref[...]
    cross_ref[...] = spread_times_window(answer, window_ref[...]) * (1.0 / CAP)


def column_norms(mean):
    parts = mean.shape[0] // RESPONSE_COUNT
    cube = mean.reshape(parts, RESPONSE_COUNT, mean.shape[1])
    return cube, jnp.sqrt(jnp.sum(cube * cube, axis=1))


def shrunk(cube, norms, level):
    return cube * (jnp.maximum(norms - level, 0.0) / jnp.maximum(norms, level))[:, None, :]


def join_halves(core, own_ref, other_ref, full_ref):
    half = own_ref.shape[0]
    full_ref[pl.ds(pl.multiple_of(core * half, half), half), :] = own_ref[...]
    full_ref[pl.ds(pl.multiple_of((1 - core) * half, half), half), :] = other_ref[...]


def next_kernel(
    own_ref,
    other_ref,
    window_ref,
    first_ref,
    second_ref,
    cross_ref,
    along_ref,
    state_ref,
    send_ref,
    keep_ref,
    *state_refs,
):
    later_ref, mean_ref = state_refs if len(state_refs) == 2 else state_refs * 2
    core, _, _ = place()
    join_halves(core, own_ref, other_ref, mean_ref)
    cube, norms = column_norms(mean_ref[...])
    level = shrink_level * (jnp.sum(norms, keepdims=True) / norms.size)
    consensus = shrunk(cube, norms, level).reshape(mean_ref.shape)
    dual = state_ref[...] - consensus
    target = cross_ref[...] + ridge_weight * (consensus - dual)
    window = window_ref[...]
    samples = first_ref.shape[0]
    projected = gathered_lags(nt_dot(target.astype(bf16), window), samples) * (1.0 / CAP)
    weights = times_matrix(projected, first_ref[...], second_ref[...])
    kept = padded(weights.astype(bf16).astype(f32), window.shape[0]) * along_ref[...]
    local = (target - spread_times_window(kept, window)) / ridge_weight
    store_halves(core, local + dual, later_ref, send_ref, keep_ref)


def part_kernel(boots, own_ref, other_ref, window_ref, support_ref, *refs):
    piece_refs, (tally_ref, full_ref, blocks_ref) = refs[:boots], refs[boots:]
    core, _, position = place()
    join_halves(core, own_ref, other_ref, full_ref)
    cube, norms = column_norms(full_ref[...])
    level = shrink_level * (jnp.sum(norms, keepdims=True) / norms.size)
    for d in range(boots):
        blocks_ref[lax.bitwise_xor(position, d)] = support_ref[d * boots : (d + 1) * boots, :]
    channels = full_ref.shape[1]
    width = blocks_ref.shape[2]
    each = channels // width
    chosen, tally = [], []
    for lag in range(LAGS):
        blocks = [blocks_ref.at[lag * each + k] for k in range(each)]
        chosen.append(jnp.concatenate([b[pl.ds(position, 1), :] for b in blocks], axis=1))
        tally.append(
            jnp.concatenate([jnp.sum(b[...], axis=0, keepdims=True) for b in blocks], axis=1)
        )
    chosen = jnp.concatenate(chosen, axis=0)[:, None, :]
    tally = jnp.maximum(jnp.concatenate(tally, axis=0), 1.0)[:, None, :]
    tally_ref[...] = jnp.sum(blocks_ref[position], axis=0, keepdims=True)
    weighted = chosen * shrunk(cube, norms, level)
    full_ref[...] = weighted.reshape(full_ref.shape)
    share = (weighted / tally).reshape(full_ref.shape).astype(bf16)
    half = RESPONSE_COUNT // 2
    samples = (piece_refs[0].shape[1] - width) // 2
    forecast = gathered_lags(nt_dot(share, window_ref[...]), samples).astype(bf16)
    for d in range(boots):
        opening = lax.bitwise_xor(position, d) * width
        row = lax.div(opening, channels) * RESPONSE_COUNT + core * half
        rows = pl.ds(pl.multiple_of(row, half), half)
        if width == channels:
            block = full_ref[rows, :]
        else:
            column = pl.multiple_of(lax.rem(opening, channels), width)
            block = full_ref[rows, pl.ds(column, width)]
        piece_refs[d][:, :width] = block.astype(bf16)
        piece_refs[d][:, width : width + samples] = forecast[:half]
        piece_refs[d][:, width + samples :] = forecast[half:]


def average_kernel(*refs):
    *piece_refs, tally_ref, averaged_ref = refs
    width = averaged_ref.shape[1]
    added = paired_sum([ref[:, :width].astype(f32) for ref in piece_refs])
    averaged_ref[...] = added / jnp.maximum(tally_ref[...], 1.0)


def residual_kernel(*refs):
    *piece_refs, answer_ref, residual_ref = refs
    half = answer_ref.shape[0] // 2
    samples = answer_ref.shape[1]
    start = piece_refs[0].shape[1] - 2 * samples
    added = paired_sum([ref[:, start:].astype(f32) for ref in piece_refs])
    residual_ref[:half, :] = answer_ref[:half, :] - added[:, :samples]
    residual_ref[half:, :] = answer_ref[half:, :] - added[:, samples:]


def last_kernel(own_ref, other_ref, averaged_ref):
    core, _, _ = place()
    join_halves(core, own_ref, other_ref, averaged_ref)


def shaped(shape, dtype=f32):
    return jax.ShapeDtypeStruct(shape, dtype)


def called(kernel, outs, ins, scratch=(), cost=None, room=32):
    return pl.pallas_call(
        kernel,
        cost_estimate=cost,
        out_shape=outs,
        in_specs=ins,
        out_specs=jax.tree.map(lambda _: VMEM, outs),
        scratch_shapes=scratch,
        compiler_params=pltpu.CompilerParams(vmem_limit_bytes=room * 1024 * 1024),
    )


def per_device(recording, starts, lengths, support):
    shards = lax.axis_size("tm")
    boots = lax.axis_size("boot")
    samples, channels = recording.shape
    width = samples + MARGIN
    rows = LAGS * RESPONSE_COUNT
    half = rows // 2
    half_shape = shaped((half, channels))
    full_shape = shaped((rows, channels))

    recording, packet, along, down = called(
        power_kernel,
        (
            shaped((samples, channels), bf16),
            shaped((8, channels)),
            shaped((1, width)),
            shaped((samples, 128)),
        ),
        [HBM] * 3,
        [
            pltpu.SMEM(starts.shape, jnp.int32),
            pltpu.SMEM(lengths.shape, jnp.int32),
            pltpu.SemaphoreType.DMA((CHUNKS + 2,)),
        ],
        room=32,
    )(*[pltpu.with_memory_space_constraint(a, pltpu.HBM) for a in (starts, lengths, recording)])
    other = swapped(packet, "tm", 1)
    direct = shards <= 8
    merged = called(
        merge_kernel, shaped((8, channels), bf16 if direct else f32), [VMEM, VMEM]
    )(packet, other)
    if direct:
        powers = chip_parts(merged)
        halos = [other] + powers[1:]
    else:
        powers = [chip_parts_sum(merged)]
        halos = [lax.ppermute(packet, "tm", [(i, i + 1) for i in range(shards - 1)])]

    square = shaped((samples, samples), bf16)
    window, high, low, bound, answer, state, send, keep = called(
        functools.partial(first_kernel, samples * shards, len(powers), len(halos)),
        (
            shaped((width, channels), bf16),
            square,
            square,
            shaped((8, 128)),
            shaped((RESPONSE_COUNT, samples)),
            full_shape,
            half_shape,
            half_shape,
        ),
        [VMEM] * (len(powers) + len(halos) + 3),
        [pltpu.VMEM((width // 128, samples + HALO, 128), f32)] * 2,
    )(*powers, *halos, recording, along, down)

    total = jnp.zeros((half, channels), f32)
    held = total
    support = support.astype(f32)
    reach = 1
    for count in range(1, ITERS + 1):
        change = (keep + swapped(send, "tm", 1) - held).astype(bf16)
        if count < ITERS:
            change, support, window, high = lax.optimization_barrier(
                (change, support, window, high)
            )
        total = total + chip_parts_sum(change)
        held = held + change.astype(f32)
        mean = total / shards
        if count == ITERS:
            break
        while reach < boots:
            support = jnp.concatenate([support, swapped(support, "boot", reach)], axis=0)
            reach *= 2
            if count + 1 < ITERS:
                break
        if count == 1:
            cross, first, second = called(
                side_kernel,
                (full_shape, square, square),
                [VMEM] * 6,
                cost=pl.CostEstimate(
                    flops=14 * samples**3, bytes_accessed=1 << 20, transcendentals=0
                ),
            )(window, high, low, bound, answer, along)
        mean, support = lax.optimization_barrier((mean, support))
        going = count + 1 < ITERS
        send, keep, *states = called(
            next_kernel,
            (half_shape, half_shape) + (full_shape,) * going,
            [VMEM] * 8,
            [pltpu.VMEM((rows, channels), f32)],
        )(mean, swapped(mean, "tm", 1), window, first, second, cross, along, state)
        state = states[0] if going else None

    features = LAGS * channels // boots
    piece = shaped((RESPONSE_COUNT // 2, features + 2 * samples), bf16)
    *pieces, tally = called(
        functools.partial(part_kernel, boots),
        (piece,) * boots + (shaped((1, features)),),
        [VMEM] * 4,
        [pltpu.VMEM((rows, channels), f32), pltpu.VMEM((boots, boots, features), f32)],
    )(mean, swapped(mean, "tm", 1), window, support)
    pieces = pieces[:1] + [swapped(pieces[d], "boot", d) for d in range(1, boots)]
    averaged = called(
        average_kernel, shaped((RESPONSE_COUNT // 2, features)), [VMEM] * (boots + 1)
    )(*pieces, tally)
    residual = called(
        residual_kernel, shaped((RESPONSE_COUNT, samples)), [VMEM] * (boots + 1)
    )(*pieces, answer)
    averaged = called(last_kernel, shaped((RESPONSE_COUNT, features)), [VMEM] * 2)(
        averaged, swapped(averaged, "tm", 1)
    )
    return averaged, residual


def solution(mesh):
    in_specs = (P("tm", None), P("boot", "tm"), P("boot", "tm"), P(None, "boot"))
    out_specs = (P(None, "boot"), P(None, "tm"))
    return jax.shard_map(
        per_device,
        mesh=mesh,
        in_specs=in_specs,
        out_specs=out_specs,
        check_vma=False,
    )
```

```python
import functools

import jax
import jax.numpy as jnp
from jax import lax
from jax.experimental import pallas as pl
from jax.experimental.pallas import tpu as pltpu
from jax.sharding import PartitionSpec as P


LAGS = 4
RESPONSE_COUNT = 32
NBLK = 6
CAP = 384
ITERS = 3
CHEB = 5

ridge_weight = 4.0
shrink_level = 0.75
epsilon = 1e-05

MARGIN = 128
HALO = 16
CHUNKS = 4


VMEM = pl.BlockSpec(memory_space=pltpu.VMEM)
HBM = pl.BlockSpec(memory_space=pltpu.HBM)
f32 = jnp.float32
bf16 = jnp.bfloat16


def swapped(block, axis, distance):
    devices = range(lax.axis_size(axis))
    return lax.ppermute(block, axis, [(i, i ^ distance) for i in devices])


def paired_sum(parts):
    while len(parts) > 1:
        parts = [parts[i] + parts[i + 1] for i in range(0, len(parts), 2)]
    return parts[0]


def chip_parts(block, step=2):
    reach = min(4, lax.axis_size("tm") // step)
    return [block] + [swapped(block, "tm", k * step) for k in range(1, reach)]


def chip_parts_sum(block):
    step = 2
    while step < lax.axis_size("tm"):
        parts = chip_parts(block, step)
        total = paired_sum([part.astype(f32) for part in parts])
        block = total.astype(block.dtype)
        step *= len(parts)
    return total


def rotated(values, shift, axis):
    return pltpu.roll(values, shift, axis)


def nt_dot(a, b):
    return lax.dot_general(a, b, (((1,), (1,)), ((), ())), preferred_element_type=f32)


def nn_dot(a, b):
    return jnp.dot(a, b, preferred_element_type=f32)


def split(values):
    high = values.astype(bf16)
    low = (values - high.astype(f32)).astype(bf16)
    return high, low


def gathered_lags(products, samples):
    rows = products.shape[0] // LAGS
    total = None
    for lag in range(LAGS):
        part = rotated(products[lag * rows : (lag + 1) * rows], 1 + lag, 1)
        total = part if total is None else total + part
    return total[:, :samples]


def spread_times_window(values, window):
    width = window.shape[0]
    lagged = jnp.concatenate(
        [rotated(values, width - 1 - lag, 1) for lag in range(LAGS)], axis=0
    )
    high, low = split(lagged)
    both = nn_dot(jnp.concatenate([high, low], axis=0), window)
    return both[: lagged.shape[0]] + both[lagged.shape[0] :]


def padded(values, width):
    rows, samples = values.shape
    return jnp.concatenate([values, jnp.zeros((rows, width - samples), f32)], axis=1)


def chebyshev(high, low, rhs, bound):
    center = ridge_weight + 0.5 * bound
    radius = 0.5 * bound
    sigma = center / radius
    answer = jnp.zeros_like(rhs)
    remain = rhs
    factor = 1.0 / sigma
    update = rhs / center
    for count in range(CHEB):
        answer = answer + update
        if count + 1 < CHEB:
            product = times_matrix(update, high, low)
            remain = remain - (ridge_weight * update + product)
            after = 1.0 / (2.0 * sigma - factor)
            update = after * factor * update + 2.0 * after / radius * remain
            factor = after
    return answer


def times_matrix(values, high, low):
    rows = values.shape[0]
    first, second = split(values)
    both = nn_dot(jnp.concatenate([first, second], axis=0), high)
    return both[:rows] + (both[rows:] + nn_dot(first, low))


def solving_matrix(weighted, bound):
    center = ridge_weight + 0.5 * bound
    radius = 0.5 * bound
    sigma = center / radius
    factors = [1.0 / sigma]
    for _ in range(CHEB - 1):
        factors.append(1.0 / (2.0 * sigma - factors[-1]))
    ratios = [None] * CHEB + [1.0]
    for k in reversed(range(CHEB)):
        ratios[k] = factors[k] * ratios[k + 1]
    g0, g1, g2, g3, g4, _ = ratios
    b4 = 2.0 * g0 / radius
    b3 = 4.0 * g1 / radius
    b2 = (4.0 * g2 + 2.0 * g0) / radius
    b1 = (4.0 * g3 + 4.0 * g1) / radius
    b0 = (2.0 * g4 + 2.0 * g2 + g0) / radius
    row = lax.broadcasted_iota(jnp.int32, weighted.shape, 0)
    column = lax.broadcasted_iota(jnp.int32, weighted.shape, 1)
    unit = jnp.where(row == column, 1.0, 0.0)
    t1 = unit - weighted * (1.0 / radius)
    high, low = split(t1)
    t2 = 2.0 * (nn_dot(high, high) + (nn_dot(low, high) + nn_dot(high, low))) - unit
    high, low = split(t2)
    first, second = split(b3 * t1 + b4 * t2)
    product = nn_dot(first, high) + (nn_dot(second, high) + nn_dot(first, low))
    return (b0 - b4) * unit + (b1 - b3) * t1 + b2 * t2 + 2.0 * product


def store_halves(core, values, state_ref, send_ref, keep_ref):
    state_ref[...] = values
    half = values.shape[0] // 2
    keep_ref[...] = state_ref[pl.ds(pl.multiple_of(core * half, half), half), :]
    send_ref[...] = state_ref[pl.ds(pl.multiple_of((1 - core) * half, half), half), :]


def uses_along(iota, starts_ref, lengths_ref):
    total = jnp.zeros(iota.shape, f32)
    for block in range(NBLK):
        begin = starts_ref[0, block]
        inside = (iota >= begin) & (iota < begin + lengths_ref[0, block])
        total = total + jnp.where(inside, 1.0, 0.0)
    return total


def place():
    index = lax.axis_index("tm")
    return lax.rem(index, 2), lax.div(index, 2), lax.axis_index("boot")


def power_kernel(
    starts_hbm,
    lengths_hbm,
    source_ref,
    recording_ref,
    packet_ref,
    along_ref,
    down_ref,
    starts_ref,
    lengths_ref,
    sems,
):
    samples, channels = source_ref.shape
    chunk = samples // CHUNKS
    plan = [
        pltpu.make_async_copy(starts_hbm, starts_ref, sems.at[CHUNKS]),
        pltpu.make_async_copy(lengths_hbm, lengths_ref, sems.at[CHUNKS + 1]),
    ]
    for copy in plan:
        copy.start()
    copies = []
    for k in range(CHUNKS):
        piece = pl.ds(k * chunk, chunk)
        copies.append(
            pltpu.make_async_copy(source_ref.at[piece], recording_ref.at[piece], sems.at[k])
        )
        copies[-1].start()
    for copy in plan:
        copy.wait()
    along_ref[...] = uses_along(
        lax.broadcasted_iota(jnp.int32, along_ref.shape, 1), starts_ref, lengths_ref
    )
    down_ref[...] = uses_along(
        lax.broadcasted_iota(jnp.int32, down_ref.shape, 0), starts_ref, lengths_ref
    )
    total = jnp.zeros((8, channels), f32)
    for k in range(CHUNKS):
        copies[k].wait()
        values = recording_ref[k * chunk : (k + 1) * chunk, :].astype(f32)
        total = total + jnp.sum((values * values).reshape(chunk // 8, 8, channels), axis=0)
    power = jnp.sum(total, axis=0, keepdims=True)
    last = recording_ref[samples - HALO :, :].astype(f32)[HALO - 8 :]
    row = lax.broadcasted_iota(jnp.int32, (8, channels), 0)
    packet_ref[...] = jnp.where(row < 8 - LAGS, power, last)


def merge_kernel(own_ref, other_ref, merged_ref):
    core, _, _ = place()
    own, other = own_ref[...], other_ref[...]
    row = lax.broadcasted_iota(jnp.int32, own.shape, 0)
    power = own + other
    first = power.astype(merged_ref.dtype).astype(f32)
    second = (power - first).astype(merged_ref.dtype).astype(f32)
    pieces = jnp.where(row == 0, first, jnp.where(row == 1, second, power - first - second))
    last = jnp.where(core == 1, own, other)
    packet = jnp.where(row < 3, pieces, jnp.where(row < 8 - LAGS, 0.0, last))
    merged_ref[...] = packet.astype(merged_ref.dtype)


def preceding_rows(refs):
    if len(refs) == 1:
        return refs[0][...]
    core, chip, _ = place()
    other_ref, *chip_refs = refs
    rows = chip_refs[0][...].astype(f32)
    if len(chip_refs) == 3:
        rows = jnp.where(chip == 2, chip_refs[2][...].astype(f32), rows)
    rows = jnp.where(core == 1, other_ref[...], rows)
    return jnp.where(core + chip > 0, rows, 0.0)


def moved_lanes(blocks, shift):
    turned = [rotated(block, shift, 1) for block in blocks]
    lane = lax.broadcasted_iota(jnp.int32, turned[0].shape, 1)
    return [jnp.where(lane < shift, turned[k - 1], turned[k]) for k in range(len(turned))]


def lagged_gram(window_ref, pairs_ref, sums_ref):
    width = window_ref.shape[0]
    count, rows, lanes = pairs_ref.shape
    samples = rows - HALO
    left = jnp.concatenate([window_ref[width - HALO :, :], window_ref[:samples, :]], axis=0)
    for k in [count - 1] + list(range(0, count - 1, 2)):
        wide = 1 if k == count - 1 else 2
        pairs = nt_dot(left, window_ref[k * lanes : (k + wide) * lanes, :])
        for i in range(wide):
            pairs_ref[k + i] = pairs[:, i * lanes : (i + 1) * lanes]
    body = rows - 8
    earlier = moved_lanes([pairs_ref[k, 7 : 7 + body, :] for k in range(count)], 1)
    for k in range(count):
        sums_ref[k, 8:, :] = pairs_ref[k, 8:, :] + earlier[k]
    first = moved_lanes([sums_ref[k, HALO - 1 : rows - 1, :] for k in range(count)], 1)
    later = moved_lanes([sums_ref[k, HALO - 3 : rows - 3, :] for k in range(count)], 3)
    return jnp.concatenate(
        [first[k] + later[k] for k in range(samples // lanes)], axis=1
    )


def first_kernel(count, parts, halos, *refs):
    part_refs, refs = refs[:parts], refs[parts:]
    halo_refs, refs = refs[:halos], refs[halos:]
    (
        recording_ref,
        along_ref,
        down_ref,
        window_ref,
        high_ref,
        low_ref,
        bound_ref,
        answer_ref,
        state_ref,
        send_ref,
        keep_ref,
        pairs_ref,
        sums_ref,
    ) = refs
    samples, channels = recording_ref.shape
    width = window_ref.shape[0]
    packets = [ref[...].astype(f32) for ref in part_refs]
    power = paired_sum([packet[:1] + packet[1:2] + packet[2:3] for packet in packets])
    scale = 1.0 / jnp.sqrt(power / count + epsilon)
    window_ref[:samples, :] = (recording_ref[...].astype(f32) * scale).astype(bf16)
    window_ref[samples : width - HALO, :] = jnp.zeros((width - HALO - samples, channels), bf16)
    row = lax.broadcasted_iota(jnp.int32, (8, channels), 0)
    tail = jnp.where(row >= 8 - LAGS, preceding_rows(halo_refs) * scale, 0.0)
    window_ref[width - HALO :, :] = jnp.concatenate(
        [jnp.zeros((HALO - 8, channels), f32), tail], axis=0
    ).astype(bf16)
    window = window_ref[...]

    along = along_ref[...]
    gram = lagged_gram(window_ref, pairs_ref, sums_ref) * (1.0 / CAP)
    weighted = gram * down_ref[:, :1]
    squares = jnp.sum(weighted * gram, axis=0, keepdims=True) * along[:, :samples]
    bound = jnp.sqrt(jnp.sum(squares, axis=1, keepdims=True))
    bound_ref[...] = jnp.broadcast_to(bound, bound_ref.shape)
    high, low = split(weighted)
    high_ref[...] = high
    low_ref[...] = low

    answer = window_ref[:samples, :128].astype(f32).T[:RESPONSE_COUNT]
    answer_ref[...] = answer
    short = answer.astype(bf16)
    projected = (nn_dot(short, high) + nn_dot(short, low)) * (1.0 / CAP)
    weights = chebyshev(high, low, projected, bound).astype(bf16).astype(f32)
    kept = padded(answer * (1.0 / CAP) - weights, width) * along
    local = spread_times_window(kept, window) / ridge_weight
    core, _, _ = place()
    store_halves(core, local, state_ref, send_ref, keep_ref)


def side_kernel(
    window_ref,
    high_ref,
    low_ref,
    bound_ref,
    answer_ref,
    along_ref,
    cross_ref,
    first_ref,
    second_ref,
    turned_ref,
):
    width = window_ref.shape[0]
    turned_ref[...] = window_ref[...].T
    weighted = high_ref[...].astype(f32) + low_ref[...].astype(f32)
    first_ref[...], second_ref[...] = split(solving_matrix(weighted, bound_ref[:1, :1]))
    answer = padded(answer_ref[...], width) * along_ref[...]
    cross_ref[...] = spread_times_window(answer, window_ref[...]) * (1.0 / CAP)


def column_norms(mean):
    parts = mean.shape[0] // RESPONSE_COUNT
    cube = mean.reshape(parts, RESPONSE_COUNT, mean.shape[1])
    return cube, jnp.sqrt(jnp.sum(cube * cube, axis=1))


def shrunk(cube, norms, level):
    return cube * (jnp.maximum(norms - level, 0.0) / jnp.maximum(norms, level))[:, None, :]


def join_halves(core, own_ref, other_ref, full_ref):
    half = own_ref.shape[0]
    full_ref[pl.ds(pl.multiple_of(core * half, half), half), :] = own_ref[...]
    full_ref[pl.ds(pl.multiple_of((1 - core) * half, half), half), :] = other_ref[...]


def next_kernel(
    own_ref,
    other_ref,
    window_ref,
    turned_ref,
    first_ref,
    second_ref,
    cross_ref,
    along_ref,
    state_ref,
    send_ref,
    keep_ref,
    *state_refs,
):
    later_ref, mean_ref = state_refs if len(state_refs) == 2 else state_refs * 2
    core, _, _ = place()
    join_halves(core, own_ref, other_ref, mean_ref)
    cube, norms = column_norms(mean_ref[...])
    level = shrink_level * (jnp.sum(norms, keepdims=True) / norms.size)
    consensus = shrunk(cube, norms, level).reshape(mean_ref.shape)
    dual = state_ref[...] - consensus
    target = cross_ref[...] + ridge_weight * (consensus - dual)
    window = window_ref[...]
    samples = first_ref.shape[0]
    products = nn_dot(target.astype(bf16), turned_ref[...])
    projected = gathered_lags(products, samples) * (1.0 / CAP)
    weights = times_matrix(projected, first_ref[...], second_ref[...])
    kept = padded(weights.astype(bf16).astype(f32), window.shape[0]) * along_ref[...]
    local = (target - spread_times_window(kept, window)) / ridge_weight
    store_halves(core, local + dual, later_ref, send_ref, keep_ref)


def part_kernel(boots, own_ref, other_ref, turned_ref, support_ref, *refs):
    piece_refs, (tally_ref, full_ref, blocks_ref) = refs[:boots], refs[boots:]
    core, _, position = place()
    join_halves(core, own_ref, other_ref, full_ref)
    cube, norms = column_norms(full_ref[...])
    level = shrink_level * (jnp.sum(norms, keepdims=True) / norms.size)
    for d in range(boots):
        blocks_ref[lax.bitwise_xor(position, d)] = support_ref[d * boots : (d + 1) * boots, :]
    channels = full_ref.shape[1]
    width = blocks_ref.shape[2]
    each = channels // width
    chosen, tally = [], []
    for lag in range(LAGS):
        blocks = [blocks_ref.at[lag * each + k] for k in range(each)]
        chosen.append(jnp.concatenate([b[pl.ds(position, 1), :] for b in blocks], axis=1))
        tally.append(
            jnp.concatenate([jnp.sum(b[...], axis=0, keepdims=True) for b in blocks], axis=1)
        )
    chosen = jnp.concatenate(chosen, axis=0)[:, None, :]
    tally = jnp.maximum(jnp.concatenate(tally, axis=0), 1.0)[:, None, :]
    tally_ref[...] = jnp.sum(blocks_ref[position], axis=0, keepdims=True)
    weighted = chosen * shrunk(cube, norms, level)
    full_ref[...] = weighted.reshape(full_ref.shape)
    share = (weighted / tally).reshape(full_ref.shape).astype(bf16)
    half = RESPONSE_COUNT // 2
    samples = (piece_refs[0].shape[1] - width) // 2
    forecast = gathered_lags(nn_dot(share, turned_ref[...]), samples).astype(bf16)
    for d in range(boots):
        opening = lax.bitwise_xor(position, d) * width
        row = lax.div(opening, channels) * RESPONSE_COUNT + core * half
        rows = pl.ds(pl.multiple_of(row, half), half)
        if width == channels:
            block = full_ref[rows, :]
        else:
            column = pl.multiple_of(lax.rem(opening, channels), width)
            block = full_ref[rows, pl.ds(column, width)]
        piece_refs[d][:, :width] = block.astype(bf16)
        piece_refs[d][:, width : width + samples] = forecast[:half]
        piece_refs[d][:, width + samples :] = forecast[half:]


def average_kernel(*refs):
    *piece_refs, tally_ref, averaged_ref = refs
    width = averaged_ref.shape[1]
    added = paired_sum([ref[:, :width].astype(f32) for ref in piece_refs])
    averaged_ref[...] = added / jnp.maximum(tally_ref[...], 1.0)


def residual_kernel(*refs):
    *piece_refs, answer_ref, residual_ref = refs
    half = answer_ref.shape[0] // 2
    samples = answer_ref.shape[1]
    start = piece_refs[0].shape[1] - 2 * samples
    added = paired_sum([ref[:, start:].astype(f32) for ref in piece_refs])
    residual_ref[:half, :] = answer_ref[:half, :] - added[:, :samples]
    residual_ref[half:, :] = answer_ref[half:, :] - added[:, samples:]


def last_kernel(own_ref, other_ref, averaged_ref):
    core, _, _ = place()
    join_halves(core, own_ref, other_ref, averaged_ref)


def shaped(shape, dtype=f32):
    return jax.ShapeDtypeStruct(shape, dtype)


def called(kernel, outs, ins, scratch=(), cost=None, room=32):
    return pl.pallas_call(
        kernel,
        cost_estimate=cost,
        out_shape=outs,
        in_specs=ins,
        out_specs=jax.tree.map(lambda _: VMEM, outs),
        scratch_shapes=scratch,
        compiler_params=pltpu.CompilerParams(vmem_limit_bytes=room * 1024 * 1024),
    )


def per_device(recording, starts, lengths, support):
    shards = lax.axis_size("tm")
    boots = lax.axis_size("boot")
    samples, channels = recording.shape
    width = samples + MARGIN
    rows = LAGS * RESPONSE_COUNT
    half = rows // 2
    half_shape = shaped((half, channels))
    full_shape = shaped((rows, channels))

    recording, packet, along, down = called(
        power_kernel,
        (
            shaped((samples, channels), bf16),
            shaped((8, channels)),
            shaped((1, width)),
            shaped((samples, 128)),
        ),
        [HBM] * 3,
        [
            pltpu.SMEM(starts.shape, jnp.int32),
            pltpu.SMEM(lengths.shape, jnp.int32),
            pltpu.SemaphoreType.DMA((CHUNKS + 2,)),
        ],
        room=32,
    )(*[pltpu.with_memory_space_constraint(a, pltpu.HBM) for a in (starts, lengths, recording)])
    other = swapped(packet, "tm", 1)
    direct = shards <= 8
    merged = called(
        merge_kernel, shaped((8, channels), bf16 if direct else f32), [VMEM, VMEM]
    )(packet, other)
    if direct:
        powers = chip_parts(merged)
        halos = [other] + powers[1:]
    else:
        powers = [chip_parts_sum(merged)]
        halos = [lax.ppermute(packet, "tm", [(i, i + 1) for i in range(shards - 1)])]

    square = shaped((samples, samples), bf16)
    window, high, low, bound, answer, state, send, keep = called(
        functools.partial(first_kernel, samples * shards, len(powers), len(halos)),
        (
            shaped((width, channels), bf16),
            square,
            square,
            shaped((8, 128)),
            shaped((RESPONSE_COUNT, samples)),
            full_shape,
            half_shape,
            half_shape,
        ),
        [VMEM] * (len(powers) + len(halos) + 3),
        [pltpu.VMEM((width // 128, samples + HALO, 128), f32)] * 2,
    )(*powers, *halos, recording, along, down)

    total = jnp.zeros((half, channels), f32)
    held = total
    support = support.astype(f32)
    reach = 1
    for count in range(1, ITERS + 1):
        change = (keep + swapped(send, "tm", 1) - held).astype(bf16)
        if count < ITERS:
            change, support, window, high = lax.optimization_barrier(
                (change, support, window, high)
            )
        total = total + chip_parts_sum(change)
        held = held + change.astype(f32)
        mean = total / shards
        if count == ITERS:
            break
        while reach < boots:
            support = jnp.concatenate([support, swapped(support, "boot", reach)], axis=0)
            reach *= 2
            if count + 1 < ITERS:
                break
        if count == 1:
            cross, first, second, turned = called(
                side_kernel,
                (full_shape, square, square, shaped((channels, width), bf16)),
                [VMEM] * 6,
                cost=pl.CostEstimate(
                    flops=14 * samples**3, bytes_accessed=1 << 20, transcendentals=0
                ),
            )(window, high, low, bound, answer, along)
        mean, support = lax.optimization_barrier((mean, support))
        going = count + 1 < ITERS
        send, keep, *states = called(
            next_kernel,
            (half_shape, half_shape) + (full_shape,) * going,
            [VMEM] * 9,
            [pltpu.VMEM((rows, channels), f32)],
        )(mean, swapped(mean, "tm", 1), window, turned, first, second, cross, along, state)
        state = states[0] if going else None

    features = LAGS * channels // boots
    piece = shaped((RESPONSE_COUNT // 2, features + 2 * samples), bf16)
    *pieces, tally = called(
        functools.partial(part_kernel, boots),
        (piece,) * boots + (shaped((1, features)),),
        [VMEM] * 4,
        [pltpu.VMEM((rows, channels), f32), pltpu.VMEM((boots, boots, features), f32)],
    )(mean, swapped(mean, "tm", 1), turned, support)
    pieces = pieces[:1] + [swapped(pieces[d], "boot", d) for d in range(1, boots)]
    averaged = called(
        average_kernel, shaped((RESPONSE_COUNT // 2, features)), [VMEM] * (boots + 1)
    )(*pieces, tally)
    residual = called(
        residual_kernel, shaped((RESPONSE_COUNT, samples)), [VMEM] * (boots + 1)
    )(*pieces, answer)
    averaged = called(last_kernel, shaped((RESPONSE_COUNT, features)), [VMEM] * 2)(
        averaged, swapped(averaged, "tm", 1)
    )
    return averaged, residual


def solution(mesh):
    in_specs = (P("tm", None), P("boot", "tm"), P("boot", "tm"), P(None, "boot"))
    out_specs = (P(None, "boot"), P(None, "tm"))
    return jax.shard_map(
        per_device,
        mesh=mesh,
        in_specs=in_specs,
        out_specs=out_specs,
        check_vma=False,
    )
```

```python
import functools

import jax
import jax.numpy as jnp
from jax import lax
from jax.experimental import pallas as pl
from jax.experimental.pallas import tpu as pltpu
from jax.sharding import PartitionSpec as P


LAGS = 4
RESPONSE_COUNT = 32
NBLK = 6
CAP = 384
ITERS = 3
CHEB = 5

ridge_weight = 4.0
shrink_level = 0.75
epsilon = 1e-05

MARGIN = 128
HALO = 16
CHUNKS = 4


VMEM = pl.BlockSpec(memory_space=pltpu.VMEM)
HBM = pl.BlockSpec(memory_space=pltpu.HBM)
f32 = jnp.float32
bf16 = jnp.bfloat16


def swapped(block, axis, distance):
    devices = range(lax.axis_size(axis))
    return lax.ppermute(block, axis, [(i, i ^ distance) for i in devices])


def paired_sum(parts):
    while len(parts) > 1:
        parts = [parts[i] + parts[i + 1] for i in range(0, len(parts), 2)]
    return parts[0]


def chip_parts(block, step=2):
    reach = min(4, lax.axis_size("tm") // step)
    return [block] + [swapped(block, "tm", k * step) for k in range(1, reach)]


def chip_parts_sum(block):
    step = 2
    while step < lax.axis_size("tm"):
        parts = chip_parts(block, step)
        total = paired_sum([part.astype(f32) for part in parts])
        block = total.astype(block.dtype)
        step *= len(parts)
    return total


def rotated(values, shift, axis):
    return pltpu.roll(values, shift, axis)


def nt_dot(a, b):
    return lax.dot_general(a, b, (((1,), (1,)), ((), ())), preferred_element_type=f32)


def nn_dot(a, b):
    return jnp.dot(a, b, preferred_element_type=f32)


def split(values):
    high = values.astype(bf16)
    low = (values - high.astype(f32)).astype(bf16)
    return high, low


def gathered_lags(products, samples):
    rows = products.shape[0] // LAGS
    total = None
    for lag in range(LAGS):
        part = rotated(products[lag * rows : (lag + 1) * rows], 1 + lag, 1)
        total = part if total is None else total + part
    return total[:, :samples]


def spread_times_window(values, window):
    width = window.shape[0]
    lagged = jnp.concatenate(
        [rotated(values, width - 1 - lag, 1) for lag in range(LAGS)], axis=0
    )
    high, low = split(lagged)
    both = nn_dot(jnp.concatenate([high, low], axis=0), window)
    return both[: lagged.shape[0]] + both[lagged.shape[0] :]


def padded(values, width):
    rows, samples = values.shape
    return jnp.concatenate([values, jnp.zeros((rows, width - samples), f32)], axis=1)


def chebyshev(high, low, rhs, bound):
    center = ridge_weight + 0.5 * bound
    radius = 0.5 * bound
    sigma = center / radius
    answer = jnp.zeros_like(rhs)
    remain = rhs
    factor = 1.0 / sigma
    update = rhs / center
    for count in range(CHEB):
        answer = answer + update
        if count + 1 < CHEB:
            product = times_matrix(update, high, low)
            remain = remain - (ridge_weight * update + product)
            after = 1.0 / (2.0 * sigma - factor)
            update = after * factor * update + 2.0 * after / radius * remain
            factor = after
    return answer


def times_matrix(values, high, low):
    rows = values.shape[0]
    first, second = split(values)
    both = nn_dot(jnp.concatenate([first, second], axis=0), high)
    return both[:rows] + (both[rows:] + nn_dot(first, low))


def solving_matrix(weighted, bound):
    center = ridge_weight + 0.5 * bound
    radius = 0.5 * bound
    sigma = center / radius
    factors = [1.0 / sigma]
    for _ in range(CHEB - 1):
        factors.append(1.0 / (2.0 * sigma - factors[-1]))
    ratios = [None] * CHEB + [1.0]
    for k in reversed(range(CHEB)):
        ratios[k] = factors[k] * ratios[k + 1]
    g0, g1, g2, g3, g4, _ = ratios
    b4 = 2.0 * g0 / radius
    b3 = 4.0 * g1 / radius
    b2 = (4.0 * g2 + 2.0 * g0) / radius
    b1 = (4.0 * g3 + 4.0 * g1) / radius
    b0 = (2.0 * g4 + 2.0 * g2 + g0) / radius
    row = lax.broadcasted_iota(jnp.int32, weighted.shape, 0)
    column = lax.broadcasted_iota(jnp.int32, weighted.shape, 1)
    unit = jnp.where(row == column, 1.0, 0.0)
    t1 = unit - weighted * (1.0 / radius)
    high, low = split(t1)
    t2 = 2.0 * (nn_dot(high, high) + (nn_dot(low, high) + nn_dot(high, low))) - unit
    high, low = split(t2)
    first, second = split(b3 * t1 + b4 * t2)
    product = nn_dot(first, high) + (nn_dot(second, high) + nn_dot(first, low))
    return (b0 - b4) * unit + (b1 - b3) * t1 + b2 * t2 + 2.0 * product


def store_halves(core, values, state_ref, send_ref, keep_ref):
    state_ref[...] = values
    half = values.shape[0] // 2
    keep_ref[...] = state_ref[pl.ds(pl.multiple_of(core * half, half), half), :]
    send_ref[...] = state_ref[pl.ds(pl.multiple_of((1 - core) * half, half), half), :]


def uses_along(iota, starts_ref, lengths_ref):
    total = jnp.zeros(iota.shape, f32)
    for block in range(NBLK):
        begin = starts_ref[0, block]
        inside = (iota >= begin) & (iota < begin + lengths_ref[0, block])
        total = total + jnp.where(inside, 1.0, 0.0)
    return total


def place():
    index = lax.axis_index("tm")
    return lax.rem(index, 2), lax.div(index, 2), lax.axis_index("boot")


def power_kernel(
    starts_hbm,
    lengths_hbm,
    source_ref,
    recording_ref,
    packet_ref,
    along_ref,
    down_ref,
    starts_ref,
    lengths_ref,
    sems,
):
    samples, channels = source_ref.shape
    chunk = samples // CHUNKS
    plan = [
        pltpu.make_async_copy(starts_hbm, starts_ref, sems.at[CHUNKS]),
        pltpu.make_async_copy(lengths_hbm, lengths_ref, sems.at[CHUNKS + 1]),
    ]
    for copy in plan:
        copy.start()
    copies = []
    for k in range(CHUNKS):
        piece = pl.ds(k * chunk, chunk)
        copies.append(
            pltpu.make_async_copy(source_ref.at[piece], recording_ref.at[piece], sems.at[k])
        )
        copies[-1].start()
    for copy in plan:
        copy.wait()
    along_ref[...] = uses_along(
        lax.broadcasted_iota(jnp.int32, along_ref.shape, 1), starts_ref, lengths_ref
    )
    down_ref[...] = uses_along(
        lax.broadcasted_iota(jnp.int32, down_ref.shape, 0), starts_ref, lengths_ref
    )
    total = jnp.zeros((8, channels), f32)
    for k in range(CHUNKS):
        copies[k].wait()
        values = recording_ref[k * chunk : (k + 1) * chunk, :].astype(f32)
        total = total + jnp.sum((values * values).reshape(chunk // 8, 8, channels), axis=0)
    power = jnp.sum(total, axis=0, keepdims=True)
    last = recording_ref[samples - HALO :, :].astype(f32)[HALO - 8 :]
    row = lax.broadcasted_iota(jnp.int32, (8, channels), 0)
    packet_ref[...] = jnp.where(row < 8 - LAGS, power, last)


def merge_kernel(own_ref, other_ref, merged_ref):
    core, _, _ = place()
    own, other = own_ref[...], other_ref[...]
    row = lax.broadcasted_iota(jnp.int32, own.shape, 0)
    power = own + other
    first = power.astype(merged_ref.dtype).astype(f32)
    second = (power - first).astype(merged_ref.dtype).astype(f32)
    pieces = jnp.where(row == 0, first, jnp.where(row == 1, second, power - first - second))
    last = jnp.where(core == 1, own, other)
    packet = jnp.where(row < 3, pieces, jnp.where(row < 8 - LAGS, 0.0, last))
    merged_ref[...] = packet.astype(merged_ref.dtype)


def preceding_rows(refs):
    if len(refs) == 1:
        return refs[0][...]
    core, chip, _ = place()
    other_ref, *chip_refs = refs
    rows = chip_refs[0][...].astype(f32)
    if len(chip_refs) == 3:
        rows = jnp.where(chip == 2, chip_refs[2][...].astype(f32), rows)
    rows = jnp.where(core == 1, other_ref[...], rows)
    return jnp.where(core + chip > 0, rows, 0.0)


def moved_lanes(blocks, shift):
    turned = [rotated(block, shift, 1) for block in blocks]
    lane = lax.broadcasted_iota(jnp.int32, turned[0].shape, 1)
    return [jnp.where(lane < shift, turned[k - 1], turned[k]) for k in range(len(turned))]


def lagged_gram(window_ref, pairs_ref, sums_ref):
    width = window_ref.shape[0]
    count, rows, lanes = pairs_ref.shape
    samples = rows - HALO
    left = jnp.concatenate([window_ref[width - HALO :, :], window_ref[:samples, :]], axis=0)
    for k in [count - 1] + list(range(0, count - 1, 2)):
        wide = 1 if k == count - 1 else 2
        pairs = nt_dot(left, window_ref[k * lanes : (k + wide) * lanes, :])
        for i in range(wide):
            pairs_ref[k + i] = pairs[:, i * lanes : (i + 1) * lanes]
    body = rows - 8
    earlier = moved_lanes([pairs_ref[k, 7 : 7 + body, :] for k in range(count)], 1)
    for k in range(count):
        sums_ref[k, 8:, :] = pairs_ref[k, 8:, :] + earlier[k]
    first = moved_lanes([sums_ref[k, HALO - 1 : rows - 1, :] for k in range(count)], 1)
    later = moved_lanes([sums_ref[k, HALO - 3 : rows - 3, :] for k in range(count)], 3)
    return jnp.concatenate(
        [first[k] + later[k] for k in range(samples // lanes)], axis=1
    )


def first_kernel(count, parts, halos, *refs):
    part_refs, refs = refs[:parts], refs[parts:]
    halo_refs, refs = refs[:halos], refs[halos:]
    (
        recording_ref,
        along_ref,
        down_ref,
        window_ref,
        high_ref,
        low_ref,
        cross_ref,
        bound_ref,
        answer_ref,
        state_ref,
        send_ref,
        keep_ref,
        pairs_ref,
        sums_ref,
    ) = refs
    samples, channels = recording_ref.shape
    width = window_ref.shape[0]
    packets = [ref[...].astype(f32) for ref in part_refs]
    power = paired_sum([packet[:1] + packet[1:2] + packet[2:3] for packet in packets])
    scale = 1.0 / jnp.sqrt(power / count + epsilon)
    window_ref[:samples, :] = (recording_ref[...].astype(f32) * scale).astype(bf16)
    window_ref[samples : width - HALO, :] = jnp.zeros((width - HALO - samples, channels), bf16)
    row = lax.broadcasted_iota(jnp.int32, (8, channels), 0)
    tail = jnp.where(row >= 8 - LAGS, preceding_rows(halo_refs) * scale, 0.0)
    window_ref[width - HALO :, :] = jnp.concatenate(
        [jnp.zeros((HALO - 8, channels), f32), tail], axis=0
    ).astype(bf16)
    window = window_ref[...]

    along = along_ref[...]
    gram = lagged_gram(window_ref, pairs_ref, sums_ref) * (1.0 / CAP)
    weighted = gram * down_ref[:, :1]
    squares = jnp.sum(weighted * gram, axis=0, keepdims=True) * along[:, :samples]
    bound = jnp.sqrt(jnp.sum(squares, axis=1, keepdims=True))
    bound_ref[...] = jnp.broadcast_to(bound, bound_ref.shape)
    high, low = split(weighted)
    high_ref[...] = high
    low_ref[...] = low

    answer = window_ref[:samples, :128].astype(f32).T[:RESPONSE_COUNT]
    answer_ref[...] = answer
    cross = spread_times_window(padded(answer, width) * along, window) * (1.0 / CAP)
    cross_ref[...] = cross
    products = nt_dot(cross.astype(bf16), window)
    projected = gathered_lags(products, samples) * (1.0 / CAP)
    weights = chebyshev(high, low, projected, bound).astype(bf16).astype(f32)
    back = spread_times_window(padded(weights, width) * along, window)
    local = (cross - back) / ridge_weight
    core, _, _ = place()
    store_halves(core, local, state_ref, send_ref, keep_ref)


def side_kernel(window_ref, high_ref, low_ref, bound_ref, first_ref, second_ref, turned_ref):
    turned_ref[...] = window_ref[...].T
    weighted = high_ref[...].astype(f32) + low_ref[...].astype(f32)
    first_ref[...], second_ref[...] = split(solving_matrix(weighted, bound_ref[:1, :1]))


def column_norms(mean):
    parts = mean.shape[0] // RESPONSE_COUNT
    cube = mean.reshape(parts, RESPONSE_COUNT, mean.shape[1])
    return cube, jnp.sqrt(jnp.sum(cube * cube, axis=1))


def shrunk(cube, norms, level):
    return cube * (jnp.maximum(norms - level, 0.0) / jnp.maximum(norms, level))[:, None, :]


def join_halves(core, own_ref, other_ref, full_ref):
    half = own_ref.shape[0]
    full_ref[pl.ds(pl.multiple_of(core * half, half), half), :] = own_ref[...]
    full_ref[pl.ds(pl.multiple_of((1 - core) * half, half), half), :] = other_ref[...]


def next_kernel(
    own_ref,
    other_ref,
    window_ref,
    turned_ref,
    first_ref,
    second_ref,
    cross_ref,
    along_ref,
    state_ref,
    send_ref,
    keep_ref,
    *state_refs,
):
    later_ref, mean_ref = state_refs if len(state_refs) == 2 else state_refs * 2
    core, _, _ = place()
    join_halves(core, own_ref, other_ref, mean_ref)
    cube, norms = column_norms(mean_ref[...])
    level = shrink_level * (jnp.sum(norms, keepdims=True) / norms.size)
    consensus = shrunk(cube, norms, level).reshape(mean_ref.shape)
    dual = state_ref[...] - consensus
    target = cross_ref[...] + ridge_weight * (consensus - dual)
    window = window_ref[...]
    samples = first_ref.shape[0]
    products = nn_dot(target.astype(bf16), turned_ref[...])
    projected = gathered_lags(products, samples) * (1.0 / CAP)
    weights = times_matrix(projected, first_ref[...], second_ref[...])
    kept = padded(weights.astype(bf16).astype(f32), window.shape[0]) * along_ref[...]
    local = (target - spread_times_window(kept, window)) / ridge_weight
    store_halves(core, local + dual, later_ref, send_ref, keep_ref)


def part_kernel(boots, own_ref, other_ref, turned_ref, support_ref, *refs):
    piece_refs, (tally_ref, full_ref, blocks_ref) = refs[:boots], refs[boots:]
    core, _, position = place()
    join_halves(core, own_ref, other_ref, full_ref)
    cube, norms = column_norms(full_ref[...])
    level = shrink_level * (jnp.sum(norms, keepdims=True) / norms.size)
    for d in range(boots):
        blocks_ref[lax.bitwise_xor(position, d)] = support_ref[d * boots : (d + 1) * boots, :]
    channels = full_ref.shape[1]
    width = blocks_ref.shape[2]
    each = channels // width
    chosen, tally = [], []
    for lag in range(LAGS):
        blocks = [blocks_ref.at[lag * each + k] for k in range(each)]
        chosen.append(jnp.concatenate([b[pl.ds(position, 1), :] for b in blocks], axis=1))
        tally.append(
            jnp.concatenate([jnp.sum(b[...], axis=0, keepdims=True) for b in blocks], axis=1)
        )
    chosen = jnp.concatenate(chosen, axis=0)[:, None, :]
    tally = jnp.maximum(jnp.concatenate(tally, axis=0), 1.0)[:, None, :]
    tally_ref[...] = jnp.sum(blocks_ref[position], axis=0, keepdims=True)
    weighted = chosen * shrunk(cube, norms, level)
    full_ref[...] = weighted.reshape(full_ref.shape)
    share = (weighted / tally).reshape(full_ref.shape).astype(bf16)
    half = RESPONSE_COUNT // 2
    samples = (piece_refs[0].shape[1] - width) // 2
    forecast = gathered_lags(nn_dot(share, turned_ref[...]), samples).astype(bf16)
    for d in range(boots):
        opening = lax.bitwise_xor(position, d) * width
        row = lax.div(opening, channels) * RESPONSE_COUNT + core * half
        rows = pl.ds(pl.multiple_of(row, half), half)
        if width == channels:
            block = full_ref[rows, :]
        else:
            column = pl.multiple_of(lax.rem(opening, channels), width)
            block = full_ref[rows, pl.ds(column, width)]
        piece_refs[d][:, :width] = block.astype(bf16)
        piece_refs[d][:, width : width + samples] = forecast[:half]
        piece_refs[d][:, width + samples :] = forecast[half:]


def average_kernel(*refs):
    *piece_refs, tally_ref, averaged_ref = refs
    width = averaged_ref.shape[1]
    added = paired_sum([ref[:, :width].astype(f32) for ref in piece_refs])
    averaged_ref[...] = added / jnp.maximum(tally_ref[...], 1.0)


def residual_kernel(*refs):
    *piece_refs, answer_ref, residual_ref = refs
    half = answer_ref.shape[0] // 2
    samples = answer_ref.shape[1]
    start = piece_refs[0].shape[1] - 2 * samples
    added = paired_sum([ref[:, start:].astype(f32) for ref in piece_refs])
    residual_ref[:half, :] = answer_ref[:half, :] - added[:, :samples]
    residual_ref[half:, :] = answer_ref[half:, :] - added[:, samples:]


def last_kernel(own_ref, other_ref, averaged_ref):
    core, _, _ = place()
    join_halves(core, own_ref, other_ref, averaged_ref)


def shaped(shape, dtype=f32):
    return jax.ShapeDtypeStruct(shape, dtype)


def called(kernel, outs, ins, scratch=(), cost=None, room=32):
    return pl.pallas_call(
        kernel,
        cost_estimate=cost,
        out_shape=outs,
        in_specs=ins,
        out_specs=jax.tree.map(lambda _: VMEM, outs),
        scratch_shapes=scratch,
        compiler_params=pltpu.CompilerParams(vmem_limit_bytes=room * 1024 * 1024),
    )


def per_device(recording, starts, lengths, support):
    shards = lax.axis_size("tm")
    boots = lax.axis_size("boot")
    samples, channels = recording.shape
    width = samples + MARGIN
    rows = LAGS * RESPONSE_COUNT
    half = rows // 2
    half_shape = shaped((half, channels))
    full_shape = shaped((rows, channels))

    recording, packet, along, down = called(
        power_kernel,
        (
            shaped((samples, channels), bf16),
            shaped((8, channels)),
            shaped((1, width)),
            shaped((samples, 128)),
        ),
        [HBM] * 3,
        [
            pltpu.SMEM(starts.shape, jnp.int32),
            pltpu.SMEM(lengths.shape, jnp.int32),
            pltpu.SemaphoreType.DMA((CHUNKS + 2,)),
        ],
        room=32,
    )(*[pltpu.with_memory_space_constraint(a, pltpu.HBM) for a in (starts, lengths, recording)])
    other = swapped(packet, "tm", 1)
    direct = shards <= 8
    merged = called(
        merge_kernel, shaped((8, channels), bf16 if direct else f32), [VMEM, VMEM]
    )(packet, other)
    if direct:
        powers = chip_parts(merged)
        halos = [other] + powers[1:]
    else:
        powers = [chip_parts_sum(merged)]
        halos = [lax.ppermute(packet, "tm", [(i, i + 1) for i in range(shards - 1)])]

    square = shaped((samples, samples), bf16)
    window, high, low, cross, bound, answer, state, send, keep = called(
        functools.partial(first_kernel, samples * shards, len(powers), len(halos)),
        (
            shaped((width, channels), bf16),
            square,
            square,
            full_shape,
            shaped((8, 128)),
            shaped((RESPONSE_COUNT, samples)),
            full_shape,
            half_shape,
            half_shape,
        ),
        [VMEM] * (len(powers) + len(halos) + 3),
        [pltpu.VMEM((width // 128, samples + HALO, 128), f32)] * 2,
    )(*powers, *halos, recording, along, down)

    total = jnp.zeros((half, channels), f32)
    held = total
    support = support.astype(f32)
    reach = 1
    for count in range(1, ITERS + 1):
        change = (keep + swapped(send, "tm", 1) - held).astype(bf16)
        if count < ITERS:
            change, support, window, high = lax.optimization_barrier(
                (change, support, window, high)
            )
        total = total + chip_parts_sum(change)
        held = held + change.astype(f32)
        mean = total / shards
        if count == ITERS:
            break
        while reach < boots:
            support = jnp.concatenate([support, swapped(support, "boot", reach)], axis=0)
            reach *= 2
            if count + 1 < ITERS:
                break
        if count == 1:
            first, second, turned = called(
                side_kernel,
                (square, square, shaped((channels, width), bf16)),
                [VMEM] * 4,
                cost=pl.CostEstimate(
                    flops=14 * samples**3, bytes_accessed=1 << 20, transcendentals=0
                ),
            )(window, high, low, bound)
        mean, support = lax.optimization_barrier((mean, support))
        going = count + 1 < ITERS
        send, keep, *states = called(
            next_kernel,
            (half_shape, half_shape) + (full_shape,) * going,
            [VMEM] * 9,
            [pltpu.VMEM((rows, channels), f32)],
        )(mean, swapped(mean, "tm", 1), window, turned, first, second, cross, along, state)
        state = states[0] if going else None

    features = LAGS * channels // boots
    piece = shaped((RESPONSE_COUNT // 2, features + 2 * samples), bf16)
    *pieces, tally = called(
        functools.partial(part_kernel, boots),
        (piece,) * boots + (shaped((1, features)),),
        [VMEM] * 4,
        [pltpu.VMEM((rows, channels), f32), pltpu.VMEM((boots, boots, features), f32)],
    )(mean, swapped(mean, "tm", 1), turned, support)
    pieces = pieces[:1] + [swapped(pieces[d], "boot", d) for d in range(1, boots)]
    averaged = called(
        average_kernel, shaped((RESPONSE_COUNT // 2, features)), [VMEM] * (boots + 1)
    )(*pieces, tally)
    residual = called(
        residual_kernel, shaped((RESPONSE_COUNT, samples)), [VMEM] * (boots + 1)
    )(*pieces, answer)
    averaged = called(last_kernel, shaped((RESPONSE_COUNT, features)), [VMEM] * 2)(
        averaged, swapped(averaged, "tm", 1)
    )
    return averaged, residual


def solution(mesh):
    in_specs = (P("tm", None), P("boot", "tm"), P("boot", "tm"), P(None, "boot"))
    out_specs = (P(None, "boot"), P(None, "tm"))
    return jax.shard_map(
        per_device,
        mesh=mesh,
        in_specs=in_specs,
        out_specs=out_specs,
        check_vma=False,
    )
```
